32 devices in a mesh: slab: 2 (over x), freq: 4 (over y, core), energy: 4 (over z).
Axes of the slice: x: 2, y: 2, z: 4, core: 2. Of those that a mesh axis runs over, the one named last changes fastest.
Arguments:
- lesser: bfloat16 [8, 4, 2, 512, 512], P('energy', 'slab'), may hold values from -6 to 6
- retarded: bfloat16 [8, 4, 2, 512, 512], P('energy', 'slab'), may hold values from -0.25 to 0.25
- coupling: bfloat16 [8, 512, 512], P('freq'), may hold values from -0.125 to 0.125
- occupations: float32 [8], P('freq'), may hold values from 0.1 to 3
- offsets: int32 [8], P('freq'), may hold values from 1 to 2
- intersection: float32 [4], P('slab'), may hold values from 0.2 to 0.6
Outputs:
- updated: float32 [8, 4, 2, 512, 512], P('energy', 'slab', None, 'freq')
The draws below stay inside these ranges and needn't reach their ends.
All inputs are finite; a program needn't handle non-finite values.
Results may differ from the reference program's by a relative error of at most 0.017.
Values may be sent and summed in bfloat16 or wider, within the bound.
A program may use at most 128 MiB of HBM per device.

```python
import math
import jax
import jax.numpy as jnp
from jax import lax

NO = 512
OFFMAX = 2
FQ_DEV = 2
ENERGIES = 8
FREQS = 8
SLABS = 4
N_FREQ = 4


def place_ends(drawn, own_key, least, top_value):
    index_at = [jax.random.randint(jax.random.fold_in(own_key, axis), (), 0, length) for axis, length in enumerate(drawn.shape)]
    widest = drawn.shape.index(max(drawn.shape))
    neighbour = index_at[:widest] + [(index_at[widest] + 1) % drawn.shape[widest]] + index_at[widest + 1:]
    return drawn.at[tuple(index_at)].set(least).at[tuple(neighbour)].set(top_value)


def levels(key, shape, cuts, low, top_value):
    def one(dim, shards_of):
        heights = jax.random.uniform(jax.random.fold_in(jax.random.fold_in(key, 6), dim), (shards_of,), jnp.float32, low / len(cuts), top_value / len(cuts))
        return jnp.repeat(jnp.exp(heights), shape[dim] // shards_of).reshape((-1,) + (1,) * (len(shape) - dim - 1))

    factor_of = one(*cuts[0])
    for cut in cuts[1:]:
        factor_of = factor_of * one(*cut)
    return factor_of


def gaussian(own_key, shape, spread, bound, cuts=(), kind=jnp.bfloat16):
    drawn = jax.random.normal(own_key, shape, jnp.float32) * spread
    if len(cuts) > 0:
        drawn = levels(own_key, shape, cuts, -0.22, 0.18) * drawn
    return jnp.clip(drawn, min=-bound, max=bound).astype(kind)


def setup_inputs(seed: int = 0) -> dict:
    splits = jax.random.split(jax.random.key(seed), 7)
    return {
        "lesser": gaussian(splits[0], (ENERGIES, SLABS, 2, NO, NO), 1.0, 6.0, ((0, 4), (1, 2))),
        "retarded": gaussian(splits[1], (ENERGIES, SLABS, 2, NO, NO), NO ** -0.5, 0.25, ((0, 4), (1, 2))),
        "coupling": gaussian(splits[2], (FREQS, NO, NO), (4 * NO) ** -0.5, 0.125, ((0, 4),)),
        "occupations": jnp.clip(jnp.exp(math.log(3.0) - 3.4011974 * jax.random.uniform(splits[3], (FREQS,), jnp.float32) ** levels(splits[3], (FREQS,), ((0, 4),), -0.2, 0.2)), 0.1, 3.0),
        "offsets": place_ends(jax.random.randint(splits[4], (FREQS,), 1, OFFMAX + 1), jax.random.fold_in(splits[4], 1), 1, OFFMAX).astype(jnp.int32),
        "intersection": jnp.clip(0.2 + 0.400000021 * jax.random.uniform(splits[5], (SLABS,), jnp.float32) ** levels(splits[5], (SLABS,), ((0, 2),), -0.2, 0.2), 0.2, 0.6),
    }


def reference(lesser, retarded, coupling, occupations, offsets, intersection):
    padded = jnp.pad(lesser, ((OFFMAX, OFFMAX), (0, 0), (0, 0), (0, 0), (0, 0)))
    group_coupling = coupling.reshape(N_FREQ, FQ_DEV, NO, NO)
    group_numbers = occupations.reshape(N_FREQ, FQ_DEV)
    group_shifts = offsets.reshape(N_FREQ, FQ_DEV)

    def energy_term(energy_index):
        def group_add(accumulated, group):
            weights, numbers, shifts = group
            lower_index = (energy_index + OFFMAX - shifts).astype(jnp.int32)
            upper_index = (energy_index + OFFMAX + shifts).astype(jnp.int32)
            lower_green = jnp.take(padded, lower_index, axis=0).astype(jnp.float32)
            upper_green = jnp.take(padded, upper_index, axis=0).astype(jnp.float32)
            scale = numbers[:, None, None, None, None]
            mixture = scale * lower_green + (scale + 1.0) * upper_green
            mixture = lax.optimization_barrier(mixture.astype(jnp.bfloat16)).astype(jnp.float32)
            weights_wide = weights.astype(jnp.float32)
            left_product = jnp.einsum('fij,fscjk->fscik', weights_wide, mixture)
            left_product = lax.optimization_barrier(left_product.astype(jnp.bfloat16)).astype(jnp.float32)
            sandwich = jnp.einsum('fscik,fmk->scim', left_product, weights_wide)
            rounded = lax.optimization_barrier(sandwich.astype(jnp.bfloat16)).astype(jnp.float32)
            return accumulated + rounded, None

        initial = jnp.zeros((SLABS, 2, NO, NO), jnp.float32)
        result, unused = lax.scan(group_add, initial, (group_coupling, group_numbers, group_shifts))
        return result

    self_energy = lax.map(energy_term, jnp.arange(ENERGIES, dtype=jnp.int32))
    self_half = lax.optimization_barrier(self_energy.astype(jnp.bfloat16)).astype(jnp.float32)
    beside = jnp.pad(self_half, ((0, 0), (1, 1), (0, 0), (0, 0), (0, 0)))
    combined = self_half + intersection[None, :, None, None, None] * (beside[:, :-2] + beside[:, 2:])
    combined = lax.optimization_barrier(combined.astype(jnp.bfloat16)).astype(jnp.float32)
    green = retarded.astype(jnp.float32)
    real_green = green[:, :, 0]
    imag_green = green[:, :, 1]
    real_self = combined[:, :, 0]
    imag_self = combined[:, :, 1]

    def by_transpose(left_side, right_side):
        return jnp.einsum('esij,eskj->esik', left_side, right_side)

    real_part = by_transpose(real_self, real_green) + by_transpose(imag_self, imag_green)
    imag_part = by_transpose(imag_self, real_green) - by_transpose(real_self, imag_green)
    product = jnp.stack([real_part, imag_part], axis=2)
    product = lax.optimization_barrier(product.astype(jnp.bfloat16)).astype(jnp.float32)
    real_product = product[:, :, 0]
    imag_product = product[:, :, 1]

    def plain_product(left_side, right_side):
        return jnp.einsum('esij,esjk->esik', left_side, right_side)

    out_real = plain_product(real_green, real_product) - plain_product(imag_green, imag_product)
    out_imag = plain_product(real_green, imag_product) + plain_product(imag_green, real_product)
    return jnp.stack([out_real, out_imag], axis=2)
```

```python
import functools
import jax
import jax.numpy as jnp
from jax import lax
from jax.experimental import pallas as pl
from jax.experimental.pallas import tpu as pltpu
from jax.sharding import PartitionSpec as P

OFFMAX = 2
UNROLL = 8
PIECES = 3
BLOCKS = 4
MESH = pl.DeviceIdType.MESH
F32 = jnp.float32
BF16 = jnp.bfloat16


def with_halo(block, sides, width):
    for axis, dim in sides:
        count = lax.axis_size(axis)
        forward = [(i, i + 1) for i in range(count - 1)]
        backward = [(target, source) for source, target in forward]
        low = lax.ppermute(
            lax.slice_in_dim(block, block.shape[dim] - width, None, axis=dim), axis, forward
        )
        high = lax.ppermute(lax.slice_in_dim(block, 0, width, axis=dim), axis, backward)
        block = jnp.concatenate([low, block, high], axis=dim)
    return block


def general(lesser, retarded, coupling, occupations, offsets, intersection):
    freq_count = lax.axis_size("freq")
    row_count = lesser.shape[-1] // freq_count
    row_first = lax.axis_index("freq") * row_count
    padded = with_halo(lesser, (("energy", 0),), OFFMAX)
    energy_count = lesser.shape[0]
    positions = jnp.arange(energy_count, dtype=jnp.int32)[None, :] + OFFMAX
    lower_green = jnp.take(padded, positions - offsets[:, None], axis=0)
    upper_green = jnp.take(padded, positions + offsets[:, None], axis=0)
    scale = occupations[:, None, None, None, None, None]
    mixture = (
        scale * lower_green.astype(F32) + (scale + 1.0) * upper_green.astype(F32)
    ).astype(BF16)
    real_green = retarded[:, :, 0]
    imag_green = retarded[:, :, 1]
    real_rows = lax.dynamic_slice_in_dim(real_green, row_first, row_count, 2)
    imag_rows = lax.dynamic_slice_in_dim(imag_green, row_first, row_count, 2)
    left_product = jnp.einsum(
        "fri,fescij->fescrj", coupling, mixture, preferred_element_type=F32
    ).astype(BF16)
    self_energy = lax.psum_scatter(
        jnp.einsum(
            "fescrj,fkj->resck", left_product, coupling, preferred_element_type=F32
        ).astype(BF16),
        "freq",
        scatter_dimension=0,
        tiled=True,
    )
    beside_all = with_halo(self_energy, (("slab", 2),), 1)
    beside = beside_all[:, :, :-2].astype(F32) + beside_all[:, :, 2:].astype(F32)
    total = self_energy.astype(F32) + intersection[None, None, :, None, None] * beside
    combined = total.astype(BF16)
    real_self = combined[:, :, :, 0]
    imag_self = combined[:, :, :, 1]

    def by_transpose(left_side, right_side):
        return jnp.einsum("resj,eskj->resk", left_side, right_side, preferred_element_type=F32)

    real_part = by_transpose(real_self, real_green) + by_transpose(imag_self, imag_green)
    imag_part = by_transpose(imag_self, real_green) - by_transpose(real_self, imag_green)
    product = jnp.stack([real_part, imag_part], axis=3).astype(BF16)
    y_piece = lax.all_gather(product, "freq", axis=0, tiled=True)
    real_piece = y_piece[:, :, :, 0]
    imag_piece = y_piece[:, :, :, 1]

    def plain_product(left_side, right_side):
        return jnp.einsum("esrm,mesk->esrk", left_side, right_side, preferred_element_type=F32)

    out_real = plain_product(real_rows, real_piece) - plain_product(imag_rows, imag_piece)
    out_imag = plain_product(real_rows, imag_piece) + plain_product(imag_rows, real_piece)
    return jnp.stack([out_real, out_imag], axis=2)


def by_rows(a, b):
    return lax.dot_general(a, b, (((1,), (1,)), ((), ())), preferred_element_type=F32)


def kernel(
    chunks, energies,
    lesser, retarded, coupling, numbers, shifts, beside_weight, out,
    green, c_buf, w_buf, r_buf, left_buf, acc, edge_own, edge_other, near_own, near_other,
    comb, rows_of, middle, result,
    store_sem, local_sem, send_sem, recv_sem,
):
    nf, size, _ = coupling.shape
    cut = size // chunks
    half = size // 2
    x, q, z = lax.axis_index("slab"), lax.axis_index("freq"), lax.axis_index("energy")
    y, core = q // 2, q % 2
    outer, edge = x, 1 - x
    partner = {"freq": 2 * y + 1 - core}
    across = {"freq": 2 * (1 - y) + core}
    diagonal = {"freq": 2 * (1 - y) + 1 - core}
    opposite = {"slab": 1 - x}
    has_low, has_high = z > 0, z < energies - 1
    below = {"energy": jnp.maximum(z - 1, 0)}
    above = {"energy": jnp.minimum(z + 1, energies - 1)}
    first = core == 0
    second = core == 1
    has_to = jnp.logical_or(jnp.logical_and(first, has_high), jnp.logical_and(second, has_low))
    has_from = jnp.logical_or(jnp.logical_and(first, has_low), jnp.logical_and(second, has_high))
    along = {"energy": jnp.clip(z + 1 - 2 * core, 0, energies - 1)}

    barrier = pltpu.get_barrier_semaphore()
    peers = [(None, partner), (None, across), (None, diagonal), (None, opposite), (has_low, below), (has_high, above)]

    def under(condition, action):
        if condition is None:
            action()
        else:
            pl.when(condition)(action)

    for condition, peer in peers:
        under(condition, lambda peer=peer: pl.semaphore_signal(barrier, inc=1, device_id=peer, device_id_type=MESH))

    count = [0, 0]

    def remote(src, dst, peer):
        n = count[0]
        count[0] += 1
        return pltpu.make_async_remote_copy(
            src_ref=src, dst_ref=dst, send_sem=send_sem.at[n], recv_sem=recv_sem.at[n],
            device_id=peer, device_id_type=MESH,
        )

    def local(src, dst):
        n = count[1]
        count[1] += 1
        return pltpu.make_async_copy(src, dst, local_sem.at[n])

    def part(slot, k):
        return c_buf.at[k, :, pl.ds(slot * cut, cut)]

    pieces = [(edge, y), (outer, y), (outer, 1 - y)]
    near_slot, far_slot, own_slot = 2 * core, 2 * core + 1, 2 - 2 * core
    passed_slot, pass_to = 3 - 2 * core, 1 + 2 * core
    columns_of = [pl.ds(k * cut, cut) for k in range(chunks)]
    load_own = [
        [local(lesser.at[1 - core, s, c, :, columns_of[k]], green.at[p, k, own_slot]) for k in range(chunks)]
        for p, (s, c) in enumerate(pieces)
    ]
    load_c = [local(coupling.at[i, :, columns_of[k]], part(i, k)) for i in range(nf) for k in range(chunks)]
    load_r = [
        local(retarded.at[e, s, c], r_buf.at[e, s, :, pl.ds(c * size, size)])
        for e in range(2)
        for s in range(2)
        for c in range(2)
    ]
    for load in load_c + load_own[0]:
        load.start()

    for i in range(nf):
        number, shift = numbers[i], shifts[i]
        none = jnp.float32(0.0)
        row = [
            jnp.where(shift == 1, number, none),
            jnp.where(shift == 2, number, none),
            jnp.where(shift == 1, number + 1.0, none),
            jnp.where(shift == 2, number + 1.0, none),
        ]
        for j in range(8):
            w_buf[i, j : j + 1, :] = jnp.full((1, cut), row[j % 4], F32)

    def zero(p, k, slot):
        green[p, k, slot] = jnp.zeros((size, cut), BF16)

    for p in range(PIECES):
        for k in range(chunks):
            pl.when(jnp.logical_not(has_from))(lambda p=p, k=k: zero(p, k, near_slot))
            pl.when(jnp.logical_not(has_from))(lambda p=p, k=k: zero(p, k, far_slot))
            pl.when(jnp.logical_not(has_to))(lambda p=p, k=k: zero(p, k, passed_slot))

    greeted = 4 + sum(condition.astype(jnp.int32) for condition in (has_low, has_high))
    pl.semaphore_wait(barrier, greeted)

    sent = []

    def go(copy, condition=None):
        under(condition, copy.start)
        sent.append((condition, copy))
        return copy

    depth = size // BLOCKS
    blocks = [(k, pl.ds(r * depth, depth)) for k in range(chunks) for r in range(BLOCKS)]

    def block(slot, b):
        k, rows = blocks[b]
        return c_buf.at[k, rows, pl.ds(slot * cut, cut)]

    c_across = [go(remote(coupling.at[x, rows, columns_of[k]], block(4, b), across)) for b, (k, rows) in enumerate(blocks)]
    near, far, passed = {}, {}, {}
    for p, (s, c) in enumerate(pieces):
        for k in range(chunks):
            near[p, k] = go(remote(lesser.at[1 - core, s, c, :, columns_of[k]], green.at[p, k, near_slot], along), has_to)
            far[p, k] = go(remote(lesser.at[core, s, c, :, columns_of[k]], green.at[p, k, far_slot], along), has_to)
            passed[p, k] = remote(green.at[p, k, near_slot], green.at[p, k, pass_to], partner)
    w_in = [go(remote(w_buf.at[pl.ds(0, nf)], w_buf.at[pl.ds(nf, nf)], partner))]
    for i in range(nf):
        slot = 4 + 2 * (x if i == 0 else 1 - x)
        w_in.append(go(remote(w_buf.at[i], w_buf.at[slot], across)))
        w_in.append(go(remote(w_buf.at[i], w_buf.at[slot + 1], diagonal)))
    c_near = [go(remote(coupling.at[i, :, columns_of[k]], part(nf + i, k), partner)) for i in range(nf) for k in range(chunks)]
    for load in load_own[1] + load_own[2] + load_r:
        load.start()

    relayed = [remote(block(4, b), block(6, b), opposite) for b in range(len(blocks))]
    c_far = [remote(part(4, k), part(5, k), partner) for k in range(chunks)]
    c_rest = [remote(part(6, k), part(7, k), partner) for k in range(chunks)]

    def pump(b):
        c_across[b].wait_recv()
        go(relayed[b])
        if b % BLOCKS == BLOCKS - 1:
            go(c_far[b // BLOCKS])

    def rest(k):
        for b in range(k * BLOCKS, (k + 1) * BLOCKS):
            relayed[b].wait_recv()
        go(c_rest[k])

    def pass_on(p, k):
        pl.when(has_from)(near[p, k].wait_recv)
        go(passed[p, k], has_from)

    def arrive(p, k):
        pl.when(has_from)(far[p, k].wait_recv)
        pl.when(has_to)(passed[p, k].wait_recv)

    def left_side(p, k, start, stop):
        def body(f, carry):
            w = w_buf[f]
            mixed = w[0:1] * green[p, k, 0].astype(F32)
            for i in (1, 2, 3):
                mixed = mixed + w[i : i + 1] * green[p, k, i].astype(F32)
            columns = pl.ds(pl.multiple_of(f * cut, cut), cut)
            whole = jnp.concatenate([c_buf[h, :, columns] for h in range(chunks)], axis=1)
            left = jnp.dot(whole, mixed.astype(BF16), preferred_element_type=F32)
            left_buf[k, :, columns] = left.astype(BF16)
            return carry

        lax.fori_loop(start, stop, body, 0, unroll=min(UNROLL, stop - start))

    def right_side(k, start, stop, rows=slice(None)):
        columns = slice(start * cut, stop * cut)
        return by_rows(left_buf[k, :, columns], c_buf[k, rows, columns])

    halves = [slice(h * half, (h + 1) * half) for h in range(2)]
    to_across = [remote(edge_own.at[h], edge_other.at[h], across) for h in range(2)]
    to_beside = [remote(edge_own.at[h], near_own.at[h], opposite) for h in range(2)]
    over_across = remote(near_own.at[1], near_other.at[1], across)
    over_beside = remote(edge_other.at[0], near_other.at[0], opposite)
    to_partner = {
        (s, c, h): remote(comb.at[0, s, c, h], comb.at[1, s, c, h], partner)
        for s in range(2)
        for c in range(2)
        for h in range(2)
    }
    weight_outer, weight_edge = beside_weight[outer], beside_weight[edge]
    last = chunks - 1

    pump(0)
    pump(1)
    pass_on(0, 0)
    pump(2)
    pump(3)
    for load in load_c + load_own[0]:
        load.wait()
    for copy in w_in + c_near:
        copy.wait_recv()
    arrive(0, 0)
    left_side(0, 0, 0, 2)
    pump(4)
    left_side(0, 0, 2, 4)
    pump(5)
    acc[0] = right_side(0, 0, 4)
    pass_on(0, 1)
    rest(0)
    pump(6)
    pump(7)
    arrive(0, 1)
    left_side(0, 1, 0, 4)
    acc[0] += right_side(1, 0, 4)
    for copy in c_far:
        copy.wait_recv()
    left_side(0, 0, 4, 6)
    left_side(0, 1, 4, 6)
    acc[0] += right_side(0, 4, 6) + right_side(1, 4, 6)
    rest(1)
    pass_on(1, 0)
    for copy in c_rest:
        copy.wait_recv()
    left_side(0, 0, 6, 8)
    left_side(0, 1, 6, 8)
    for h in range(2):
        total = acc[0, :, halves[h]] + (right_side(0, 6, 8, halves[h]) + right_side(1, 6, 8, halves[h]))
        edge_own[h] = total.astype(BF16)
        go(to_across[h])
        if h == 1:
            go(to_beside[1])
            go(to_beside[0])

    for load in load_own[1] + load_own[2] + load_r:
        load.wait()
    rows = size // 4
    mine = pl.ds(pl.multiple_of(q * rows, rows), rows)
    here = y == 0
    for n, e in enumerate((core, 1 - core)):
        for m, s in enumerate((outer, edge)):
            real, imag = r_buf[e, s, mine, :size], r_buf[e, s, mine, size:]
            rows_of[n, m, 0] = jnp.concatenate([jnp.where(here, real, -imag), jnp.where(here, imag, real)], axis=0)
            rows_of[n, m, 1] = jnp.concatenate([jnp.where(here, -imag, real), jnp.where(here, real, imag)], axis=0)

    arrive(1, 0)
    left_side(1, 0, 0, 8)
    acc[1] = right_side(0, 0, 8)
    pass_on(1, 1)
    arrive(1, 1)
    left_side(1, 1, 0, 8)
    for h in range(2):
        total = acc[1, :, halves[h]] + right_side(last, 0, 8, halves[h])
        own = edge_own[h].astype(F32)
        comb[0, 0, 0, h] = (total + weight_outer * own).astype(BF16)
        go(to_partner[0, 0, h])
        acc[1, :, halves[h]] = own + weight_edge * total
    to_beside[1].wait_recv()
    go(over_across)
    to_across[0].wait_recv()
    go(over_beside)
    pass_on(2, 0)
    arrive(2, 0)
    left_side(2, 0, 0, 8)
    acc[0] = right_side(0, 0, 8)

    def project(n, m, c, h):
        return jnp.dot(rows_of[n, m, c], comb[n, m, c, h], preferred_element_type=F32)

    to_beside[0].wait_recv()
    for h in range(2):
        comb[0, 1, 0, h] = (acc[1, :, halves[h]] + weight_edge * near_own[h].astype(F32)).astype(BF16)
        go(to_partner[1, 0, h])
    pass_on(2, 1)
    for n in range(2):
        for m in range(2):
            for h in range(2):
                if n == 1:
                    to_partner[m, 0, h].wait_recv()
                middle[n, m, :, halves[h]] = project(n, m, 0, h)
    to_across[1].wait_recv()
    arrive(2, 1)
    left_side(2, 1, 0, 8)
    over_across.wait_recv()
    over_beside.wait_recv()
    for h in range(2):
        total = acc[0, :, halves[h]] + right_side(last, 0, 8, halves[h])
        other = edge_other[h].astype(F32)
        comb[0, 0, 1, h] = (total + weight_outer * other).astype(BF16)
        go(to_partner[0, 1, h])
        comb[0, 1, 1, h] = (other + weight_edge * (total + near_other[h].astype(F32))).astype(BF16)
        go(to_partner[1, 1, h])

    stores = []
    for n, e in enumerate((core, 1 - core)):
        for m, s in enumerate((outer, edge)):
            whole = []
            for h in range(2):
                if n == 1:
                    to_partner[m, 1, h].wait_recv()
                whole.append((middle[n, m, :, halves[h]] + project(n, m, 1, h)).astype(BF16))
            both = jnp.concatenate(whole, axis=1)
            real, imag = both[:rows], both[rows:]
            sides = jnp.concatenate(
                [jnp.concatenate([real, imag], axis=1), jnp.concatenate([imag, -real], axis=1)], axis=0
            )
            updated = by_rows(sides, r_buf[e, s]).astype(BF16)
            result[n, m, 0] = updated[:rows]
            result[n, m, 1] = updated[rows:]
            store = pltpu.make_async_copy(result.at[n, m], out.at[e, s], store_sem.at[n, m])
            store.start()
            stores.append(store)

    for store in stores:
        store.wait()
    for condition, copy in sent:
        under(condition, copy.wait_send)


def fast(lesser, retarded, coupling, occupations, offsets, intersection):
    nf, size, _ = coupling.shape
    chunks = 2
    cut = size // chunks
    rows = size // 4
    copies = chunks * (2 * BLOCKS + 3 * PIECES + 2 + nf) + 1 + 2 * nf + 14
    loads = PIECES * chunks + nf * chunks + 8
    anywhere = pl.BlockSpec(memory_space=pl.ANY)
    return pl.pallas_call(
        functools.partial(kernel, chunks, lax.axis_size("energy")),
        out_shape=jax.ShapeDtypeStruct((2, 2, 2, rows, size), BF16),
        in_specs=[anywhere] * 3 + [pl.BlockSpec(memory_space=pltpu.SMEM)] * 3,
        out_specs=anywhere,
        scratch_shapes=[
            pltpu.VMEM((PIECES, chunks, 4, size, cut), BF16),
            pltpu.VMEM((chunks, size, 4 * nf * cut), BF16),
            pltpu.VMEM((4 * nf, 8, cut), F32),
            pltpu.VMEM((2, 2, size, 2 * size), BF16),
            pltpu.VMEM((chunks, size, 4 * nf * cut), BF16),
            pltpu.VMEM((2, size, size), F32),
            pltpu.VMEM((2, size, size // 2), BF16),
            pltpu.VMEM((2, size, size // 2), BF16),
            pltpu.VMEM((2, size, size // 2), BF16),
            pltpu.VMEM((2, size, size // 2), BF16),
            pltpu.VMEM((2, 2, 2, 2, size, size // 2), BF16),
            pltpu.VMEM((2, 2, 2, 2 * rows, size), BF16),
            pltpu.VMEM((2, 2, 2 * rows, size), F32),
            pltpu.VMEM((2, 2, 2, rows, size), BF16),
            pltpu.SemaphoreType.DMA((2, 2)),
            pltpu.SemaphoreType.DMA((loads,)),
            pltpu.SemaphoreType.DMA((copies,)),
            pltpu.SemaphoreType.DMA((copies,)),
        ],
        compiler_params=pltpu.CompilerParams(
            collective_id=0, has_side_effects=True, vmem_limit_bytes=60 << 20
        ),
    )(lesser, retarded, coupling, occupations, offsets, intersection).astype(F32)


def solution(mesh):
    def shards(lesser, retarded, *rest):
        fits = (
            (mesh.shape["slab"], mesh.shape["freq"]) == (2, 4)
            and lesser.shape[:2] == (2, 2)
            and lesser.shape[-1] == 512
            and rest[0].shape[0] == 2
        )
        return (fast if fits else general)(lesser, retarded, *rest)

    return jax.shard_map(
        shards,
        mesh=mesh,
        in_specs=(
            P("energy", "slab", None, None, None),
            P("energy", "slab", None, None, None),
            P("freq", None, None),
            P("freq"),
            P("freq"),
            P("slab"),
        ),
        out_specs=P("energy", "slab", None, "freq", None),
        check_vma=False,
    )
```

```python
import functools
import jax
import jax.numpy as jnp
from jax import lax
from jax.experimental import pallas as pl
from jax.experimental.pallas import tpu as pltpu
from jax.sharding import PartitionSpec as P

OFFMAX = 2
UNROLL = 8
PIECES = 3
BLOCKS = 4
MESH = pl.DeviceIdType.MESH
F32 = jnp.float32
BF16 = jnp.bfloat16


def with_halo(block, sides, width):
    for axis, dim in sides:
        count = lax.axis_size(axis)
        forward = [(i, i + 1) for i in range(count - 1)]
        backward = [(target, source) for source, target in forward]
        low = lax.ppermute(
            lax.slice_in_dim(block, block.shape[dim] - width, None, axis=dim), axis, forward
        )
        high = lax.ppermute(lax.slice_in_dim(block, 0, width, axis=dim), axis, backward)
        block = jnp.concatenate([low, block, high], axis=dim)
    return block


def general(lesser, retarded, coupling, occupations, offsets, intersection):
    freq_count = lax.axis_size("freq")
    row_count = lesser.shape[-1] // freq_count
    row_first = lax.axis_index("freq") * row_count
    padded = with_halo(lesser, (("energy", 0),), OFFMAX)
    energy_count = lesser.shape[0]
    positions = jnp.arange(energy_count, dtype=jnp.int32)[None, :] + OFFMAX
    lower_green = jnp.take(padded, positions - offsets[:, None], axis=0)
    upper_green = jnp.take(padded, positions + offsets[:, None], axis=0)
    scale = occupations[:, None, None, None, None, None]
    mixture = (
        scale * lower_green.astype(F32) + (scale + 1.0) * upper_green.astype(F32)
    ).astype(BF16)
    real_green = retarded[:, :, 0]
    imag_green = retarded[:, :, 1]
    real_rows = lax.dynamic_slice_in_dim(real_green, row_first, row_count, 2)
    imag_rows = lax.dynamic_slice_in_dim(imag_green, row_first, row_count, 2)
    left_product = jnp.einsum(
        "fri,fescij->fescrj", coupling, mixture, preferred_element_type=F32
    ).astype(BF16)
    self_energy = lax.psum_scatter(
        jnp.einsum(
            "fescrj,fkj->resck", left_product, coupling, preferred_element_type=F32
        ).astype(BF16),
        "freq",
        scatter_dimension=0,
        tiled=True,
    )
    beside_all = with_halo(self_energy, (("slab", 2),), 1)
    beside = beside_all[:, :, :-2].astype(F32) + beside_all[:, :, 2:].astype(F32)
    total = self_energy.astype(F32) + intersection[None, None, :, None, None] * beside
    combined = total.astype(BF16)
    real_self = combined[:, :, :, 0]
    imag_self = combined[:, :, :, 1]

    def by_transpose(left_side, right_side):
        return jnp.einsum("resj,eskj->resk", left_side, right_side, preferred_element_type=F32)

    real_part = by_transpose(real_self, real_green) + by_transpose(imag_self, imag_green)
    imag_part = by_transpose(imag_self, real_green) - by_transpose(real_self, imag_green)
    product = jnp.stack([real_part, imag_part], axis=3).astype(BF16)
    y_piece = lax.all_gather(product, "freq", axis=0, tiled=True)
    real_piece = y_piece[:, :, :, 0]
    imag_piece = y_piece[:, :, :, 1]

    def plain_product(left_side, right_side):
        return jnp.einsum("esrm,mesk->esrk", left_side, right_side, preferred_element_type=F32)

    out_real = plain_product(real_rows, real_piece) - plain_product(imag_rows, imag_piece)
    out_imag = plain_product(real_rows, imag_piece) + plain_product(imag_rows, real_piece)
    return jnp.stack([out_real, out_imag], axis=2)


def by_rows(a, b):
    return lax.dot_general(a, b, (((1,), (1,)), ((), ())), preferred_element_type=F32)


def kernel(
    chunks, energies,
    lesser, retarded, coupling, numbers, shifts, beside_weight, out,
    green, c_buf, w_buf, r_buf, left_buf, acc, edge_own, edge_other, near_own, near_other,
    comb, rows_of, middle, result,
    store_sem, local_sem, send_sem, recv_sem,
):
    nf, size, _ = coupling.shape
    cut = size // chunks
    half = size // 2
    x, q, z = lax.axis_index("slab"), lax.axis_index("freq"), lax.axis_index("energy")
    y, core = q // 2, q % 2
    outer, edge = x, 1 - x
    partner = {"freq": 2 * y + 1 - core}
    across = {"freq": 2 * (1 - y) + core}
    diagonal = {"freq": 2 * (1 - y) + 1 - core}
    opposite = {"slab": 1 - x}
    has_low, has_high = z > 0, z < energies - 1
    below = {"energy": jnp.maximum(z - 1, 0)}
    above = {"energy": jnp.minimum(z + 1, energies - 1)}
    first = core == 0
    second = core == 1
    has_to = jnp.logical_or(jnp.logical_and(first, has_high), jnp.logical_and(second, has_low))
    has_from = jnp.logical_or(jnp.logical_and(first, has_low), jnp.logical_and(second, has_high))
    along = {"energy": jnp.clip(z + 1 - 2 * core, 0, energies - 1)}

    barrier = pltpu.get_barrier_semaphore()
    peers = [(None, partner), (None, across), (None, diagonal), (None, opposite), (has_low, below), (has_high, above)]

    def under(condition, action):
        if condition is None:
            action()
        else:
            pl.when(condition)(action)

    for condition, peer in peers:
        under(condition, lambda peer=peer: pl.semaphore_signal(barrier, inc=1, device_id=peer, device_id_type=MESH))

    count = [0, 0]

    def remote(src, dst, peer):
        n = count[0]
        count[0] += 1
        return pltpu.make_async_remote_copy(
            src_ref=src, dst_ref=dst, send_sem=send_sem.at[n], recv_sem=recv_sem.at[n],
            device_id=peer, device_id_type=MESH,
        )

    def local(src, dst):
        n = count[1]
        count[1] += 1
        return pltpu.make_async_copy(src, dst, local_sem.at[n])

    def part(slot, k):
        return c_buf.at[k, :, pl.ds(slot * cut, cut)]

    pieces = [(edge, y), (outer, y), (outer, 1 - y)]
    near_slot, far_slot, own_slot = 2 * core, 2 * core + 1, 2 - 2 * core
    passed_slot, pass_to = 3 - 2 * core, 1 + 2 * core
    columns_of = [pl.ds(k * cut, cut) for k in range(chunks)]
    load_own = [
        [local(lesser.at[1 - core, s, c, :, columns_of[k]], green.at[p, k, own_slot]) for k in range(chunks)]
        for p, (s, c) in enumerate(pieces)
    ]
    load_c = [local(coupling.at[i, :, columns_of[k]], part(i, k)) for i in range(nf) for k in range(chunks)]
    load_r = [
        local(retarded.at[e, s, c], r_buf.at[e, s, :, pl.ds(c * size, size)])
        for e in range(2)
        for s in range(2)
        for c in range(2)
    ]
    for load in load_c + load_own[0]:
        load.start()

    for i in range(nf):
        number, shift = numbers[i], shifts[i]
        none = jnp.float32(0.0)
        row = [
            jnp.where(shift == 1, number, none),
            jnp.where(shift == 2, number, none),
            jnp.where(shift == 1, number + 1.0, none),
            jnp.where(shift == 2, number + 1.0, none),
        ]
        for j in range(8):
            w_buf[i, j : j + 1, :] = jnp.full((1, cut), row[j % 4], F32)

    def zero(p, k, slot):
        green[p, k, slot] = jnp.zeros((size, cut), BF16)

    for p in range(PIECES):
        for k in range(chunks):
            pl.when(jnp.logical_not(has_from))(lambda p=p, k=k: zero(p, k, near_slot))
            pl.when(jnp.logical_not(has_from))(lambda p=p, k=k: zero(p, k, far_slot))
            pl.when(jnp.logical_not(has_to))(lambda p=p, k=k: zero(p, k, passed_slot))

    greeted = 4 + sum(condition.astype(jnp.int32) for condition in (has_low, has_high))
    pl.semaphore_wait(barrier, greeted)

    sent = []

    def go(copy, condition=None):
        under(condition, copy.start)
        sent.append((condition, copy))
        return copy

    depth = size // BLOCKS
    blocks = [(k, pl.ds(r * depth, depth)) for k in range(chunks) for r in range(BLOCKS)]

    def block(slot, b):
        k, rows = blocks[b]
        return c_buf.at[k, rows, pl.ds(slot * cut, cut)]

    w_in = [go(remote(w_buf.at[pl.ds(0, nf)], w_buf.at[pl.ds(nf, nf)], partner))]
    for i in range(nf):
        slot = 4 + 2 * (x if i == 0 else 1 - x)
        w_in.append(go(remote(w_buf.at[i], w_buf.at[slot], across)))
        w_in.append(go(remote(w_buf.at[i], w_buf.at[slot + 1], diagonal)))
    c_across = [go(remote(coupling.at[x, rows, columns_of[k]], block(4, b), across)) for b, (k, rows) in enumerate(blocks)]
    c_near = [go(remote(coupling.at[i, :, columns_of[k]], part(nf + i, k), partner)) for i in range(nf) for k in range(chunks)]
    near, far, passed = {}, {}, {}
    for p, (s, c) in enumerate(pieces):
        for k in range(chunks):
            near[p, k] = go(remote(lesser.at[1 - core, s, c, :, columns_of[k]], green.at[p, k, near_slot], along), has_to)
            far[p, k] = go(remote(lesser.at[core, s, c, :, columns_of[k]], green.at[p, k, far_slot], along), has_to)
            passed[p, k] = remote(green.at[p, k, near_slot], green.at[p, k, pass_to], partner)
    for load in load_own[1] + load_own[2] + load_r:
        load.start()

    relayed = [remote(block(4, b), block(6, b), opposite) for b in range(len(blocks))]
    c_far = [remote(part(4, k), part(5, k), partner) for k in range(chunks)]
    c_rest = [remote(part(6, k), part(7, k), partner) for k in range(chunks)]

    def pump(b):
        c_across[b].wait_recv()
        go(relayed[b])
        if b % BLOCKS == BLOCKS - 1:
            go(c_far[b // BLOCKS])

    def rest(k):
        for b in range(k * BLOCKS, (k + 1) * BLOCKS):
            relayed[b].wait_recv()
        go(c_rest[k])

    def pass_on(p, k):
        pl.when(has_from)(near[p, k].wait_recv)
        go(passed[p, k], has_from)

    def arrive(p, k):
        pl.when(has_from)(far[p, k].wait_recv)
        pl.when(has_to)(passed[p, k].wait_recv)

    def left_side(p, k, start, stop):
        def body(f, carry):
            w = w_buf[f]
            mixed = w[0:1] * green[p, k, 0].astype(F32)
            for i in (1, 2, 3):
                mixed = mixed + w[i : i + 1] * green[p, k, i].astype(F32)
            columns = pl.ds(pl.multiple_of(f * cut, cut), cut)
            whole = jnp.concatenate([c_buf[h, :, columns] for h in range(chunks)], axis=1)
            left = jnp.dot(whole, mixed.astype(BF16), preferred_element_type=F32)
            left_buf[k, :, columns] = left.astype(BF16)
            return carry

        lax.fori_loop(start, stop, body, 0, unroll=min(UNROLL, stop - start))

    def right_side(k, start, stop, rows=slice(None)):
        columns = slice(start * cut, stop * cut)
        return by_rows(left_buf[k, :, columns], c_buf[k, rows, columns])

    halves = [pl.ds(h * half, half) for h in range(2)]
    to_across = [remote(edge_own.at[:, columns], edge_other.at[:, columns], across) for columns in halves]
    to_beside = [remote(edge_own.at[:, columns], near_own.at[:, columns], opposite) for columns in halves]
    over_across = remote(near_own.at[:, halves[1]], near_other.at[:, halves[1]], across)
    over_beside = remote(edge_other.at[:, halves[0]], near_other.at[:, halves[0]], opposite)
    to_partner = {(m, c): remote(comb.at[0, m, c], comb.at[1, m, c], partner) for m in range(2) for c in range(2)}
    weight_outer, weight_edge = beside_weight[outer], beside_weight[edge]
    last = chunks - 1

    pump(0)
    pump(1)
    pass_on(0, 0)
    pump(2)
    pump(3)
    for load in load_c + load_own[0]:
        load.wait()
    for copy in w_in + c_near:
        copy.wait_recv()
    arrive(0, 0)
    left_side(0, 0, 0, 2)
    pump(4)
    left_side(0, 0, 2, 4)
    pump(5)
    acc[0] = right_side(0, 0, 4)
    pass_on(0, 1)
    rest(0)
    pump(6)
    pump(7)
    arrive(0, 1)
    left_side(0, 1, 0, 4)
    acc[0] += right_side(1, 0, 4)
    for copy in c_far:
        copy.wait_recv()
    left_side(0, 0, 4, 6)
    left_side(0, 1, 4, 6)
    acc[0] += right_side(0, 4, 6) + right_side(1, 4, 6)
    rest(1)
    pass_on(1, 0)
    for copy in c_rest:
        copy.wait_recv()
    left_side(0, 0, 6, 8)
    left_side(0, 1, 6, 8)
    edge_own[...] = (acc[0] + (right_side(0, 6, 8) + right_side(1, 6, 8))).astype(BF16)
    go(to_across[0])
    go(to_beside[1])
    go(to_across[1])
    go(to_beside[0])

    for load in load_own[1] + load_own[2] + load_r:
        load.wait()
    rows = size // 4
    mine = pl.ds(pl.multiple_of(q * rows, rows), rows)
    here = y == 0
    for n, e in enumerate((core, 1 - core)):
        for m, s in enumerate((outer, edge)):
            real, imag = r_buf[e, s, mine, :size], r_buf[e, s, mine, size:]
            rows_of[n, m, 0] = jnp.concatenate([jnp.where(here, real, -imag), jnp.where(here, imag, real)], axis=0)
            rows_of[n, m, 1] = jnp.concatenate([jnp.where(here, -imag, real), jnp.where(here, real, imag)], axis=0)

    arrive(1, 0)
    left_side(1, 0, 0, 8)
    acc[1] = right_side(0, 0, 8)
    pass_on(1, 1)
    arrive(1, 1)
    left_side(1, 1, 0, 8)
    total = acc[1] + right_side(last, 0, 8)
    own = edge_own[...].astype(F32)
    comb[0, 0, 0] = (total + weight_outer * own).astype(BF16)
    go(to_partner[0, 0])
    acc[1] = own + weight_edge * total
    to_beside[1].wait_recv()
    go(over_across)
    to_across[0].wait_recv()
    go(over_beside)
    pass_on(2, 0)
    arrive(2, 0)
    left_side(2, 0, 0, 8)
    acc[0] = right_side(0, 0, 8)

    def project(n, m, c):
        return jnp.dot(rows_of[n, m, c], comb[n, m, c], preferred_element_type=F32)

    to_beside[0].wait_recv()
    comb[0, 1, 0] = (acc[1] + weight_edge * near_own[...].astype(F32)).astype(BF16)
    go(to_partner[1, 0])
    pass_on(2, 1)
    for n in range(2):
        for m in range(2):
            if n == 1:
                to_partner[m, 0].wait_recv()
            middle[n, m] = project(n, m, 0)
    to_across[1].wait_recv()
    arrive(2, 1)
    left_side(2, 1, 0, 8)
    over_across.wait_recv()
    over_beside.wait_recv()
    total = acc[0] + right_side(last, 0, 8)
    other = edge_other[...].astype(F32)
    comb[0, 0, 1] = (total + weight_outer * other).astype(BF16)
    go(to_partner[0, 1])
    comb[0, 1, 1] = (other + weight_edge * (total + near_other[...].astype(F32))).astype(BF16)
    go(to_partner[1, 1])

    stores = []
    for n, e in enumerate((core, 1 - core)):
        for m, s in enumerate((outer, edge)):
            if n == 1:
                to_partner[m, 1].wait_recv()
            both = (middle[n, m] + project(n, m, 1)).astype(BF16)
            real, imag = both[:rows], both[rows:]
            sides = jnp.concatenate(
                [jnp.concatenate([real, imag], axis=1), jnp.concatenate([imag, -real], axis=1)], axis=0
            )
            updated = by_rows(sides, r_buf[e, s]).astype(BF16)
            result[n, m, 0] = updated[:rows]
            result[n, m, 1] = updated[rows:]
            store = pltpu.make_async_copy(result.at[n, m], out.at[e, s], store_sem.at[n, m])
            store.start()
            stores.append(store)

    for store in stores:
        store.wait()
    for condition, copy in sent:
        under(condition, copy.wait_send)


def fast(lesser, retarded, coupling, occupations, offsets, intersection):
    nf, size, _ = coupling.shape
    chunks = 2
    cut = size // chunks
    rows = size // 4
    copies = chunks * (2 * BLOCKS + 3 * PIECES + 2 + nf) + 1 + 2 * nf + 10
    loads = PIECES * chunks + nf * chunks + 8
    anywhere = pl.BlockSpec(memory_space=pl.ANY)
    return pl.pallas_call(
        functools.partial(kernel, chunks, lax.axis_size("energy")),
        out_shape=jax.ShapeDtypeStruct((2, 2, 2, rows, size), BF16),
        in_specs=[anywhere] * 3 + [pl.BlockSpec(memory_space=pltpu.SMEM)] * 3,
        out_specs=anywhere,
        scratch_shapes=[
            pltpu.VMEM((PIECES, chunks, 4, size, cut), BF16),
            pltpu.VMEM((chunks, size, 4 * nf * cut), BF16),
            pltpu.VMEM((4 * nf, 8, cut), F32),
            pltpu.VMEM((2, 2, size, 2 * size), BF16),
            pltpu.VMEM((chunks, size, 4 * nf * cut), BF16),
            pltpu.VMEM((2, size, size), F32),
            pltpu.VMEM((size, size), BF16),
            pltpu.VMEM((size, size), BF16),
            pltpu.VMEM((size, size), BF16),
            pltpu.VMEM((size, size), BF16),
            pltpu.VMEM((2, 2, 2, size, size), BF16),
            pltpu.VMEM((2, 2, 2, 2 * rows, size), BF16),
            pltpu.VMEM((2, 2, 2 * rows, size), F32),
            pltpu.VMEM((2, 2, 2, rows, size), BF16),
            pltpu.SemaphoreType.DMA((2, 2)),
            pltpu.SemaphoreType.DMA((loads,)),
            pltpu.SemaphoreType.DMA((copies,)),
            pltpu.SemaphoreType.DMA((copies,)),
        ],
        compiler_params=pltpu.CompilerParams(
            collective_id=0, has_side_effects=True, vmem_limit_bytes=60 << 20
        ),
    )(lesser, retarded, coupling, occupations, offsets, intersection).astype(F32)


def solution(mesh):
    def shards(lesser, retarded, *rest):
        fits = (
            (mesh.shape["slab"], mesh.shape["freq"]) == (2, 4)
            and lesser.shape[:2] == (2, 2)
            and lesser.shape[-1] == 512
            and rest[0].shape[0] == 2
        )
        return (fast if fits else general)(lesser, retarded, *rest)

    return jax.shard_map(
        shards,
        mesh=mesh,
        in_specs=(
            P("energy", "slab", None, None, None),
            P("energy", "slab", None, None, None),
            P("freq", None, None),
            P("freq"),
            P("freq"),
            P("slab"),
        ),
        out_specs=P("energy", "slab", None, "freq", None),
        check_vma=False,
    )
```

```python
import functools
import jax
import jax.numpy as jnp
from jax import lax
from jax.experimental import pallas as pl
from jax.experimental.pallas import tpu as pltpu
from jax.sharding import PartitionSpec as P

OFFMAX = 2
UNROLL = 8
PIECES = 3
BLOCKS = 8
GROUPS = 14
MESH = pl.DeviceIdType.MESH
F32 = jnp.float32
BF16 = jnp.bfloat16


def with_halo(block, sides, width):
    for axis, dim in sides:
        count = lax.axis_size(axis)
        forward = [(i, i + 1) for i in range(count - 1)]
        backward = [(target, source) for source, target in forward]
        low = lax.ppermute(
            lax.slice_in_dim(block, block.shape[dim] - width, None, axis=dim), axis, forward
        )
        high = lax.ppermute(lax.slice_in_dim(block, 0, width, axis=dim), axis, backward)
        block = jnp.concatenate([low, block, high], axis=dim)
    return block


def general(lesser, retarded, coupling, occupations, offsets, intersection):
    freq_count = lax.axis_size("freq")
    row_count = lesser.shape[-1] // freq_count
    row_first = lax.axis_index("freq") * row_count
    padded = with_halo(lesser, (("energy", 0),), OFFMAX)
    energy_count = lesser.shape[0]
    positions = jnp.arange(energy_count, dtype=jnp.int32)[None, :] + OFFMAX
    lower_green = jnp.take(padded, positions - offsets[:, None], axis=0)
    upper_green = jnp.take(padded, positions + offsets[:, None], axis=0)
    scale = occupations[:, None, None, None, None, None]
    mixture = (
        scale * lower_green.astype(F32) + (scale + 1.0) * upper_green.astype(F32)
    ).astype(BF16)
    real_green = retarded[:, :, 0]
    imag_green = retarded[:, :, 1]
    real_rows = lax.dynamic_slice_in_dim(real_green, row_first, row_count, 2)
    imag_rows = lax.dynamic_slice_in_dim(imag_green, row_first, row_count, 2)
    left_product = jnp.einsum(
        "fri,fescij->fescrj", coupling, mixture, preferred_element_type=F32
    ).astype(BF16)
    self_energy = lax.psum_scatter(
        jnp.einsum(
            "fescrj,fkj->resck", left_product, coupling, preferred_element_type=F32
        ).astype(BF16),
        "freq",
        scatter_dimension=0,
        tiled=True,
    )
    beside_all = with_halo(self_energy, (("slab", 2),), 1)
    beside = beside_all[:, :, :-2].astype(F32) + beside_all[:, :, 2:].astype(F32)
    total = self_energy.astype(F32) + intersection[None, None, :, None, None] * beside
    combined = total.astype(BF16)
    real_self = combined[:, :, :, 0]
    imag_self = combined[:, :, :, 1]

    def by_transpose(left_side, right_side):
        return jnp.einsum("resj,eskj->resk", left_side, right_side, preferred_element_type=F32)

    real_part = by_transpose(real_self, real_green) + by_transpose(imag_self, imag_green)
    imag_part = by_transpose(imag_self, real_green) - by_transpose(real_self, imag_green)
    product = jnp.stack([real_part, imag_part], axis=3).astype(BF16)
    y_piece = lax.all_gather(product, "freq", axis=0, tiled=True)
    real_piece = y_piece[:, :, :, 0]
    imag_piece = y_piece[:, :, :, 1]

    def plain_product(left_side, right_side):
        return jnp.einsum("esrm,mesk->esrk", left_side, right_side, preferred_element_type=F32)

    out_real = plain_product(real_rows, real_piece) - plain_product(imag_rows, imag_piece)
    out_imag = plain_product(real_rows, imag_piece) + plain_product(imag_rows, real_piece)
    return jnp.stack([out_real, out_imag], axis=2)


def by_rows(a, b):
    return lax.dot_general(a, b, (((1,), (1,)), ((), ())), preferred_element_type=F32)


def kernel(
    chunks, energies,
    lesser, retarded, coupling, numbers, shifts, beside_weight, out,
    green, c_buf, w_tile, w_buf, r_buf, left_buf, acc, edge_own, edge_other, near_own, near_other,
    comb, rows_of, middle,
    local_sem, send_sem, recv_sem,
):
    nf, size, _ = coupling.shape
    cut = size // chunks
    half = size // 2
    x, q, z = lax.axis_index("slab"), lax.axis_index("freq"), lax.axis_index("energy")
    y, core = q // 2, q % 2
    outer, edge = x, 1 - x
    partner = {"freq": 2 * y + 1 - core}
    across = {"freq": 2 * (1 - y) + core}
    diagonal = {"freq": 2 * (1 - y) + 1 - core}
    opposite = {"slab": 1 - x}
    has_low, has_high = z > 0, z < energies - 1
    below = {"energy": jnp.maximum(z - 1, 0)}
    above = {"energy": jnp.minimum(z + 1, energies - 1)}
    first = core == 0
    second = core == 1
    has_to = jnp.logical_or(jnp.logical_and(first, has_high), jnp.logical_and(second, has_low))
    has_from = jnp.logical_or(jnp.logical_and(first, has_low), jnp.logical_and(second, has_high))
    along = {"energy": jnp.clip(z + 1 - 2 * core, 0, energies - 1)}

    barrier = pltpu.get_barrier_semaphore()
    peers = [(None, partner), (None, across), (None, diagonal), (None, opposite), (has_low, below), (has_high, above)]

    def under(condition, action):
        if condition is None:
            action()
        else:
            pl.when(condition)(action)

    for condition, peer in peers:
        under(condition, lambda peer=peer: pl.semaphore_signal(barrier, inc=1, device_id=peer, device_id_type=MESH))

    count = [0]
    groups = []

    def group(total, condition=None):
        groups.append((total, condition))
        return len(groups) - 1, condition

    def remote(src, dst, peer, kind):
        n = count[0]
        count[0] += 1
        copy = pltpu.make_async_remote_copy(
            src_ref=src, dst_ref=dst, send_sem=send_sem.at[kind[0]], recv_sem=recv_sem.at[n],
            device_id=peer, device_id_type=MESH,
        )
        return copy, kind[1]

    def go(pair):
        under(pair[1], pair[0].start)
        return pair

    def came(pair):
        pair[0].wait_recv()

    pieces = [(edge, y), (outer, y), (outer, 1 - y)]
    near_slot, far_slot, own_slot = 2 * core, 2 * core + 1, 2 - 2 * core
    passed_slot, pass_to = 3 - 2 * core, 1 + 2 * core
    columns_of = [pl.ds(k * cut, cut) for k in range(chunks)]
    load_c = pltpu.make_async_copy(coupling, c_buf.at[pl.ds(0, nf)], local_sem.at[0])
    load_r = pltpu.make_async_copy(retarded, r_buf, local_sem.at[1])
    load_own = [
        pltpu.make_async_copy(lesser.at[1 - core, s, c], green.at[p, own_slot], local_sem.at[2 + p])
        for p, (s, c) in enumerate(pieces)
    ]
    load_c.start()
    load_own[0].start()

    for i in range(nf):
        number, shift = numbers[i], shifts[i]
        none = jnp.float32(0.0)
        row = [
            jnp.where(shift == 1, number, none),
            jnp.where(shift == 2, number, none),
            jnp.where(shift == 1, number + 1.0, none),
            jnp.where(shift == 2, number + 1.0, none),
        ]
        for j in range(4):
            w_tile[0, 4 * i + j : 4 * i + j + 1, :] = jnp.full((1, 128), row[j], F32)

    def zero(p, slot):
        green[p, slot] = jnp.zeros((size, size), BF16)

    def fill(p):
        pl.when(jnp.logical_not(has_from))(lambda: zero(p, near_slot))
        pl.when(jnp.logical_not(has_from))(lambda: zero(p, far_slot))
        pl.when(jnp.logical_not(has_to))(lambda: zero(p, passed_slot))

    greeted = 4 + sum(condition.astype(jnp.int32) for condition in (has_low, has_high))
    pl.semaphore_wait(barrier, greeted)

    depth = size // BLOCKS
    rows_at = [pl.ds(b * depth, depth) for b in range(BLOCKS)]
    relays = BLOCKS - 1
    for_w = group(w_tile.at[pl.ds(0, 3)])
    w_in = [go(remote(w_tile.at[0], w_tile.at[d + 1], peer, for_w)) for d, peer in enumerate((partner, across, diagonal))]
    for_across = group(c_buf.at[4])
    for_direct = group(c_buf.at[4, rows_at[relays]])
    c_across = [go(remote(coupling.at[x, rows], c_buf.at[4, rows], across, for_across)) for rows in rows_at]
    c_direct = go(remote(coupling.at[1 - x, rows_at[relays]], c_buf.at[6, rows_at[relays]], across, for_direct))
    for_z = group(green.at[:, pl.ds(0, 2)], has_to)
    for_passed = group(green.at[:, 0], has_from)
    near, far, passed = {}, {}, {}
    for_near = group(coupling)
    for p, (s, c) in enumerate(pieces):
        for k, columns in enumerate(columns_of):
            near[p, k] = go(remote(lesser.at[1 - core, s, c, :, columns], green.at[p, near_slot, :, columns], along, for_z))
            far[p, k] = go(remote(lesser.at[core, s, c, :, columns], green.at[p, far_slot, :, columns], along, for_z))
            passed[p, k] = remote(green.at[p, near_slot, :, columns], green.at[p, pass_to, :, columns], partner, for_passed)
        if p == 0:
            c_near = go(remote(coupling, c_buf.at[pl.ds(nf, nf)], partner, for_near))
    for load in load_own[1:] + [load_r]:
        load.start()

    for_relay, for_far, for_rest = group(c_buf.at[4, pl.ds(0, relays * depth)]), group(c_buf.at[4]), group(c_buf.at[6])
    relayed = [remote(c_buf.at[4, rows], c_buf.at[6, rows], opposite, for_relay) for rows in rows_at[:relays]]
    whole_halves = [pl.ds(h * half, half) for h in range(2)]
    c_far = [remote(c_buf.at[4, rows], c_buf.at[5, rows], partner, for_far) for rows in whole_halves]
    c_rest = [remote(c_buf.at[6, rows], c_buf.at[7, rows], partner, for_rest) for rows in whole_halves]

    def pump(b):
        came(c_across[b])
        if b < relays:
            go(relayed[b])
        if b == BLOCKS // 2 - 1:
            go(c_far[0])
        if b == BLOCKS - 1:
            go(c_far[1])

    def rest(h):
        for b in range(h * BLOCKS // 2, (h + 1) * BLOCKS // 2):
            came(relayed[b] if b < relays else c_direct)
        go(c_rest[h])

    def pass_on(p, k):
        pl.when(has_from)(near[p, k][0].wait_recv)
        go(passed[p, k])

    def arrive(p, k):
        pl.when(has_from)(far[p, k][0].wait_recv)
        pl.when(has_to)(passed[p, k][0].wait_recv)

    def spread():
        for slot in range(4 * nf):
            source = slot // 2 if slot < 4 else 2 + slot % 2
            for i in range(4):
                if slot < 4:
                    row = w_tile[source, 4 * (slot % 2) + i : 4 * (slot % 2) + i + 1]
                else:
                    pair = (w_tile[source, i : i + 1], w_tile[source, 4 + i : 5 + i])
                    row = jnp.where((x == 0) == (slot < 6), pair[0], pair[1])
                wide = jnp.broadcast_to(row, (16, 128)).astype(BF16)
                w_buf[slot, i] = jnp.concatenate([wide] * (size // 128), axis=1)

    def mixture(p, columns, f):
        width = columns.stop - columns.start

        def term(i):
            block = green[p, i, :, columns].reshape(size // 16, 16, width)
            return w_buf[f, i, :, columns][None] * block

        return ((term(0) + term(1)) + (term(2) + term(3))).reshape(size, width)

    def left_side(p, columns, start, stop):
        def product(f, carry):
            left = jnp.dot(c_buf[f], mixture(p, columns, f), preferred_element_type=F32)
            left_buf[f, :, columns] = left.astype(BF16)
            return carry

        lax.fori_loop(start, stop, product, 0, unroll=min(UNROLL, stop - start))

    def right_side(columns, start, stop):
        def beside(ref):
            return jnp.concatenate([ref[f, :, columns] for f in range(start, stop)], axis=1)

        return by_rows(beside(left_buf), beside(c_buf))

    part = [slice(k * cut, (k + 1) * cut) for k in range(chunks)]
    full = slice(0, size)
    halves = whole_halves
    for_edge, for_beside = group(edge_own), group(edge_own)
    to_across = [remote(edge_own.at[:, columns], edge_other.at[:, columns], across, for_edge) for columns in halves]
    to_beside = [remote(edge_own.at[:, columns], near_own.at[:, columns], opposite, for_beside) for columns in halves]
    over_across = remote(near_own.at[:, halves[1]], near_other.at[:, halves[1]], across, group(near_own.at[:, halves[1]]))
    over_beside = remote(edge_other.at[:, halves[0]], near_other.at[:, halves[0]], opposite, group(near_own.at[:, halves[1]]))
    for_comb = group(comb.at[0])
    to_partner = {
        (m, c): remote(comb.at[0, m, c], comb.at[1, m, c], partner, for_comb) for m in range(2) for c in range(2)
    }
    weight_outer, weight_edge = beside_weight[outer], beside_weight[edge]

    fill(0)
    pump(0)
    pump(1)
    pass_on(0, 0)
    pump(2)
    pump(3)
    for copy in w_in:
        came(copy)
    spread()
    load_c.wait()
    load_own[0].wait()
    came(c_near)
    arrive(0, 0)
    left_side(0, part[0], 0, 2)
    pump(4)
    left_side(0, part[0], 2, 4)
    pump(5)
    acc[0] = right_side(part[0], 0, 4)
    pass_on(0, 1)
    pump(6)
    rest(0)
    pump(7)
    arrive(0, 1)
    left_side(0, part[1], 0, 4)
    acc[0] += right_side(part[1], 0, 4)
    for copy in c_far:
        came(copy)
    left_side(0, full, 4, 6)
    rest(1)
    acc[0] += right_side(full, 4, 6)
    pass_on(1, 0)
    for copy in c_rest:
        came(copy)
    left_side(0, full, 6, 8)
    edge_own[...] = (acc[0] + right_side(full, 6, 8)).astype(BF16)
    go(to_across[0])
    go(to_beside[1])
    go(to_across[1])
    go(to_beside[0])

    fill(1)
    fill(2)
    for load in load_own[1:] + [load_r]:
        load.wait()
    rows = size // 4
    mine = pl.ds(pl.multiple_of(q * rows, rows), rows)
    here = y == 0
    for n, e in enumerate((core, 1 - core)):
        for m, s in enumerate((outer, edge)):
            real, imag = r_buf[e, s, 0, mine], r_buf[e, s, 1, mine]
            rows_of[n, m, 0] = jnp.concatenate([jnp.where(here, real, -imag), jnp.where(here, imag, real)], axis=0)
            rows_of[n, m, 1] = jnp.concatenate([jnp.where(here, -imag, real), jnp.where(here, real, imag)], axis=0)

    arrive(1, 0)
    left_side(1, part[0], 0, 8)
    acc[1] = right_side(part[0], 0, 8)
    pass_on(1, 1)
    arrive(1, 1)
    left_side(1, part[1], 0, 8)
    total = acc[1] + right_side(part[1], 0, 8)
    own = edge_own[...].astype(F32)
    comb[0, 0, 0] = (total + weight_outer * own).astype(BF16)
    go(to_partner[0, 0])
    acc[1] = own + weight_edge * total
    came(to_beside[1])
    go(over_across)
    came(to_across[0])
    go(over_beside)
    pass_on(2, 0)
    arrive(2, 0)
    left_side(2, part[0], 0, 8)
    acc[0] = right_side(part[0], 0, 8)

    def project(n, m, c):
        return jnp.dot(rows_of[n, m, c], comb[n, m, c], preferred_element_type=F32)

    came(to_beside[0])
    comb[0, 1, 0] = (acc[1] + weight_edge * near_own[...].astype(F32)).astype(BF16)
    go(to_partner[1, 0])
    pass_on(2, 1)
    for n in range(2):
        for m in range(2):
            if n == 1:
                came(to_partner[m, 0])
            middle[n, m] = project(n, m, 0)
    came(to_across[1])
    arrive(2, 1)
    left_side(2, part[1], 0, 8)
    acc[0] += right_side(part[1], 0, 8)
    comb[0, 0, 1] = (acc[0] + weight_outer * edge_other[...].astype(F32)).astype(BF16)
    go(to_partner[0, 1])

    def finish(n, m):
        e, s = (core, 1 - core)[n], (outer, edge)[m]
        if n == 1:
            came(to_partner[m, 1])
        both = (middle[n, m] + project(n, m, 1)).astype(BF16)
        real, imag = both[:rows], both[rows:]
        sides = jnp.concatenate(
            [jnp.concatenate([real, imag], axis=1), jnp.concatenate([imag, -real], axis=1)], axis=0
        )
        updated = by_rows(sides, jnp.concatenate([r_buf[e, s, 0], r_buf[e, s, 1]], axis=1))
        out[e, s, 0] = updated[:rows]
        out[e, s, 1] = updated[rows:]

    finish(0, 0)
    came(over_across)
    came(over_beside)
    around = acc[0] + near_other[...].astype(F32)
    comb[0, 1, 1] = (edge_other[...].astype(F32) + weight_edge * around).astype(BF16)
    go(to_partner[1, 1])
    finish(1, 0)
    finish(0, 1)
    finish(1, 1)

    for n, (total, condition) in enumerate(groups):
        done = pltpu.make_async_remote_copy(
            src_ref=total, dst_ref=total, send_sem=send_sem.at[n], recv_sem=recv_sem.at[0],
            device_id=partner, device_id_type=MESH,
        )
        under(condition, done.wait_send)


def fast(lesser, retarded, coupling, occupations, offsets, intersection):
    nf, size, _ = coupling.shape
    chunks = 2
    rows = size // 4
    arrivals = 3 + 1 + BLOCKS + 1 + (BLOCKS - 1) + 4 + 3 * PIECES * chunks + 6 + 4
    anywhere = pl.BlockSpec(memory_space=pl.ANY)
    return pl.pallas_call(
        functools.partial(kernel, chunks, lax.axis_size("energy")),
        out_shape=pltpu.VMEM((2, 2, 2, rows, size), F32),
        in_specs=[anywhere] * 3 + [pl.BlockSpec(memory_space=pltpu.SMEM)] * 3,
        out_specs=pl.BlockSpec(memory_space=pltpu.VMEM),
        scratch_shapes=[
            pltpu.VMEM((PIECES, 4, size, size), BF16),
            pltpu.VMEM((4 * nf, size, size), BF16),
            pltpu.VMEM((4, 8, 128), F32),
            pltpu.VMEM((4 * nf, 4, 16, size), BF16),
            pltpu.VMEM((2, 2, 2, size, size), BF16),
            pltpu.VMEM((4 * nf, size, size), BF16),
            pltpu.VMEM((2, size, size), F32),
            pltpu.VMEM((size, size), BF16),
            pltpu.VMEM((size, size), BF16),
            pltpu.VMEM((size, size), BF16),
            pltpu.VMEM((size, size), BF16),
            pltpu.VMEM((2, 2, 2, size, size), BF16),
            pltpu.VMEM((2, 2, 2, 2 * rows, size), BF16),
            pltpu.VMEM((2, 2, 2 * rows, size), F32),
            pltpu.SemaphoreType.DMA((2 + PIECES,)),
            pltpu.SemaphoreType.DMA((GROUPS,)),
            pltpu.SemaphoreType.DMA((arrivals,)),
        ],
        compiler_params=pltpu.CompilerParams(
            collective_id=0, has_side_effects=True, vmem_limit_bytes=60 << 20
        ),
    )(lesser, retarded, coupling, occupations, offsets, intersection)


def solution(mesh):
    def shards(lesser, retarded, *rest):
        fits = (
            (mesh.shape["slab"], mesh.shape["freq"]) == (2, 4)
            and lesser.shape[:2] == (2, 2)
            and lesser.shape[-1] == 512
            and rest[0].shape[0] == 2
        )
        return (fast if fits else general)(lesser, retarded, *rest)

    return jax.shard_map(
        shards,
        mesh=mesh,
        in_specs=(
            P("energy", "slab", None, None, None),
            P("energy", "slab", None, None, None),
            P("freq", None, None),
            P("freq"),
            P("freq"),
            P("slab"),
        ),
        out_specs=P("energy", "slab", None, "freq", None),
        check_vma=False,
    )
```

```python
import functools
import jax
import jax.numpy as jnp
from jax import lax
from jax.experimental import pallas as pl
from jax.experimental.pallas import tpu as pltpu
from jax.sharding import PartitionSpec as P

OFFMAX = 2
UNROLL = 8
PIECES = 3
RELAYS = (96, 96, 96, 64, 64, 32)
EARLY = 3
GROUPS = 14
MESH = pl.DeviceIdType.MESH
F32 = jnp.float32
BF16 = jnp.bfloat16


def with_halo(block, sides, width):
    for axis, dim in sides:
        count = lax.axis_size(axis)
        forward = [(i, i + 1) for i in range(count - 1)]
        backward = [(target, source) for source, target in forward]
        low = lax.ppermute(
            lax.slice_in_dim(block, block.shape[dim] - width, None, axis=dim), axis, forward
        )
        high = lax.ppermute(lax.slice_in_dim(block, 0, width, axis=dim), axis, backward)
        block = jnp.concatenate([low, block, high], axis=dim)
    return block


def general(lesser, retarded, coupling, occupations, offsets, intersection):
    freq_count = lax.axis_size("freq")
    row_count = lesser.shape[-1] // freq_count
    row_first = lax.axis_index("freq") * row_count
    padded = with_halo(lesser, (("energy", 0),), OFFMAX)
    energy_count = lesser.shape[0]
    positions = jnp.arange(energy_count, dtype=jnp.int32)[None, :] + OFFMAX
    lower_green = jnp.take(padded, positions - offsets[:, None], axis=0)
    upper_green = jnp.take(padded, positions + offsets[:, None], axis=0)
    scale = occupations[:, None, None, None, None, None]
    mixture = (
        scale * lower_green.astype(F32) + (scale + 1.0) * upper_green.astype(F32)
    ).astype(BF16)
    real_green = retarded[:, :, 0]
    imag_green = retarded[:, :, 1]
    real_rows = lax.dynamic_slice_in_dim(real_green, row_first, row_count, 2)
    imag_rows = lax.dynamic_slice_in_dim(imag_green, row_first, row_count, 2)
    left_product = jnp.einsum(
        "fri,fescij->fescrj", coupling, mixture, preferred_element_type=F32
    ).astype(BF16)
    self_energy = lax.psum_scatter(
        jnp.einsum(
            "fescrj,fkj->resck", left_product, coupling, preferred_element_type=F32
        ).astype(BF16),
        "freq",
        scatter_dimension=0,
        tiled=True,
    )
    beside_all = with_halo(self_energy, (("slab", 2),), 1)
    beside = beside_all[:, :, :-2].astype(F32) + beside_all[:, :, 2:].astype(F32)
    total = self_energy.astype(F32) + intersection[None, None, :, None, None] * beside
    combined = total.astype(BF16)
    real_self = combined[:, :, :, 0]
    imag_self = combined[:, :, :, 1]

    def by_transpose(left_side, right_side):
        return jnp.einsum("resj,eskj->resk", left_side, right_side, preferred_element_type=F32)

    real_part = by_transpose(real_self, real_green) + by_transpose(imag_self, imag_green)
    imag_part = by_transpose(imag_self, real_green) - by_transpose(real_self, imag_green)
    product = jnp.stack([real_part, imag_part], axis=3).astype(BF16)
    y_piece = lax.all_gather(product, "freq", axis=0, tiled=True)
    real_piece = y_piece[:, :, :, 0]
    imag_piece = y_piece[:, :, :, 1]

    def plain_product(left_side, right_side):
        return jnp.einsum("esrm,mesk->esrk", left_side, right_side, preferred_element_type=F32)

    out_real = plain_product(real_rows, real_piece) - plain_product(imag_rows, imag_piece)
    out_imag = plain_product(real_rows, imag_piece) + plain_product(imag_rows, real_piece)
    return jnp.stack([out_real, out_imag], axis=2)


def by_rows(a, b):
    return lax.dot_general(a, b, (((1,), (1,)), ((), ())), preferred_element_type=F32)


def kernel(
    energies,
    lesser, retarded, coupling, numbers, shifts, beside_weight, out,
    green, c_buf, w_tile, w_buf, r_buf, left_buf, acc, edge_own, edge_other, near_own, near_other,
    comb, rows_of, middle,
    local_sem, send_sem, recv_sem,
):
    nf, size, _ = coupling.shape
    half = size // 2
    x, q, z = lax.axis_index("slab"), lax.axis_index("freq"), lax.axis_index("energy")
    y, core = q // 2, q % 2
    outer, edge = x, 1 - x
    partner = {"freq": 2 * y + 1 - core}
    across = {"freq": 2 * (1 - y) + core}
    opposite = {"slab": 1 - x}
    has_low, has_high = z > 0, z < energies - 1
    first = core == 0
    second = core == 1
    has_to = jnp.logical_or(jnp.logical_and(first, has_high), jnp.logical_and(second, has_low))
    has_from = jnp.logical_or(jnp.logical_and(first, has_low), jnp.logical_and(second, has_high))
    along = {"energy": jnp.clip(z + 1 - 2 * core, 0, energies - 1)}
    behind = {"energy": jnp.clip(z - 1 + 2 * core, 0, energies - 1)}

    barrier = pltpu.get_barrier_semaphore()
    peers = [(None, partner), (None, across), (None, opposite), (has_from, behind)]

    def under(condition, action):
        if condition is None:
            action()
        else:
            pl.when(condition)(action)

    for condition, peer in peers:
        under(condition, lambda peer=peer: pl.semaphore_signal(barrier, inc=1, device_id=peer, device_id_type=MESH))

    count = [0]
    groups = []

    def group(total, condition=None):
        groups.append((total, condition))
        return len(groups) - 1, condition

    def remote(src, dst, peer, kind):
        n = count[0]
        count[0] += 1
        copy = pltpu.make_async_remote_copy(
            src_ref=src, dst_ref=dst, send_sem=send_sem.at[kind[0]], recv_sem=recv_sem.at[n],
            device_id=peer, device_id_type=MESH,
        )
        return copy, kind[1]

    def go(pair):
        under(pair[1], pair[0].start)
        return pair

    def came(pair):
        pair[0].wait_recv()

    pieces = [(edge, y), (outer, y), (outer, 1 - y)]
    near_slot, far_slot, own_slot = 2 * core, 2 * core + 1, 2 - 2 * core
    passed_slot, pass_to = 3 - 2 * core, 1 + 2 * core
    parts = [slice(0, half), slice(half, size)]
    load_c = pltpu.make_async_copy(coupling, c_buf.at[pl.ds(0, nf)], local_sem.at[0])
    load_r = pltpu.make_async_copy(retarded, r_buf, local_sem.at[1])
    load_own = [
        pltpu.make_async_copy(lesser.at[1 - core, s, c], green.at[p, own_slot], local_sem.at[2 + p])
        for p, (s, c) in enumerate(pieces)
    ]
    load_c.start()
    load_own[0].start()

    for i in range(nf):
        number, shift = numbers[i], shifts[i]
        none = jnp.float32(0.0)
        row = [
            jnp.where(shift == 1, number, none),
            jnp.where(shift == 2, number, none),
            jnp.where(shift == 1, number + 1.0, none),
            jnp.where(shift == 2, number + 1.0, none),
        ]
        for j in range(4):
            w_tile[0, 4 * i + j : 4 * i + j + 1, :] = jnp.full((1, 128), row[j], F32)

    def zero(p, slot):
        green[p, slot] = jnp.zeros((size, size), BF16)

    def fill(p):
        pl.when(jnp.logical_not(has_from))(lambda: zero(p, near_slot))
        pl.when(jnp.logical_not(has_from))(lambda: zero(p, far_slot))
        pl.when(jnp.logical_not(has_to))(lambda: zero(p, passed_slot))

    pl.semaphore_wait(barrier, 3 + has_to.astype(jnp.int32))

    starts = [sum(RELAYS[:b]) for b in range(len(RELAYS) + 1)]
    rows_at = [pl.ds(start, depth) for start, depth in zip(starts, RELAYS)]
    kept = pl.ds(starts[-1], size - starts[-1])
    staged = [pl.ds(0, starts[EARLY]), pl.ds(starts[EARLY], size - starts[EARLY])]
    for_w = group(w_tile.at[pl.ds(0, 3)])
    w_in = [go(remote(w_tile.at[0], w_tile.at[d + 1], peer, for_w)) for d, peer in enumerate((partner, across))]
    w_on = remote(w_tile.at[2], w_tile.at[3], partner, for_w)
    for_across = group(c_buf.at[4])
    for_direct = group(c_buf.at[4, kept])
    c_across = [go(remote(coupling.at[x, rows], c_buf.at[4, rows], across, for_across)) for rows in rows_at + [kept]]
    c_direct = go(remote(coupling.at[1 - x, kept], c_buf.at[6, kept], across, for_direct))
    for_z = group(green.at[:, pl.ds(0, 2)], has_to)
    for_passed = group(green.at[:, 0], has_from)
    near, far, passed = {}, {}, {}
    for_near = group(coupling)
    for p, (s, c) in enumerate(pieces):
        for k, columns in enumerate(parts):
            near[p, k] = go(remote(lesser.at[1 - core, s, c, :, columns], green.at[p, near_slot, :, columns], along, for_z))
            far[p, k] = go(remote(lesser.at[core, s, c, :, columns], green.at[p, far_slot, :, columns], along, for_z))
            passed[p, k] = remote(green.at[p, near_slot, :, columns], green.at[p, pass_to, :, columns], partner, for_passed)
        if p == 0:
            c_near = go(remote(coupling, c_buf.at[pl.ds(nf, nf)], partner, for_near))
    for load in load_own[1:] + [load_r]:
        load.start()

    for_relay, for_far, for_rest = group(c_buf.at[4, pl.ds(0, starts[-1])]), group(c_buf.at[4]), group(c_buf.at[6])
    relayed = [remote(c_buf.at[4, rows], c_buf.at[6, rows], opposite, for_relay) for rows in rows_at]
    c_far = [remote(c_buf.at[4, rows], c_buf.at[5, rows], partner, for_far) for rows in staged]
    c_rest = [remote(c_buf.at[6, rows], c_buf.at[7, rows], partner, for_rest) for rows in staged]

    def pump(b):
        came(c_across[b])
        if b < len(relayed):
            go(relayed[b])
        if b == EARLY - 1:
            go(c_far[0])
        if b == len(relayed):
            go(c_far[1])

    def rest(h):
        for copy in (relayed[EARLY:] + [c_direct]) if h else relayed[:EARLY]:
            came(copy)
        go(c_rest[h])

    def pass_on(p, k):
        pl.when(has_from)(near[p, k][0].wait_recv)
        go(passed[p, k])

    def arrive(p, k):
        pl.when(has_from)(far[p, k][0].wait_recv)
        pl.when(has_to)(passed[p, k][0].wait_recv)

    def spread():
        for slot in range(4 * nf):
            source = slot // 2 if slot < 4 else 2 + slot % 2
            for i in range(4):
                if slot < 4:
                    row = w_tile[source, 4 * (slot % 2) + i : 4 * (slot % 2) + i + 1]
                else:
                    pair = (w_tile[source, i : i + 1], w_tile[source, 4 + i : 5 + i])
                    row = jnp.where((x == 0) == (slot < 6), pair[0], pair[1])
                wide = jnp.broadcast_to(row, (16, 128)).astype(BF16)
                w_buf[slot, i] = jnp.concatenate([wide] * (size // 128), axis=1)

    def mixture(p, columns, f):
        width = columns.stop - columns.start

        def term(i):
            block = green[p, i, :, columns].reshape(size // 16, 16, width)
            return w_buf[f, i, :, columns][None] * block

        return ((term(0) + term(1)) + (term(2) + term(3))).reshape(size, width)

    def left_side(p, columns, start, stop):
        def product(f, carry):
            left = jnp.dot(c_buf[f], mixture(p, columns, f), preferred_element_type=F32)
            left_buf[f, :, columns] = left.astype(BF16)
            return carry

        lax.fori_loop(start, stop, product, 0, unroll=min(UNROLL, stop - start))

    def right_side(columns, start, stop):
        def beside(ref):
            return jnp.concatenate([ref[f, :, columns] for f in range(start, stop)], axis=1)

        return by_rows(beside(left_buf), beside(c_buf))

    full = slice(0, size)
    halves = [pl.ds(h * half, half) for h in range(2)]
    for_edge, for_beside = group(edge_own), group(edge_own)
    to_across = [remote(edge_own.at[:, columns], edge_other.at[:, columns], across, for_edge) for columns in halves]
    to_beside = [remote(edge_own.at[:, columns], near_own.at[:, columns], opposite, for_beside) for columns in halves]
    for_over, for_under = group(near_own.at[:, halves[1]]), group(near_own.at[:, halves[1]])
    over_across = [remote(near_own.at[rows, halves[1]], near_other.at[rows, halves[1]], across, for_over) for rows in halves]
    over_beside = [remote(edge_other.at[rows, halves[0]], near_other.at[rows, halves[0]], opposite, for_under) for rows in halves]
    for_comb = group(comb.at[0])
    to_partner = {(m, c): remote(comb.at[0, m, c], comb.at[1, m, c], partner, for_comb) for m, c in ((0, 0), (1, 0), (0, 1))}
    last_to_partner = [remote(comb.at[0, 1, 1, rows], comb.at[1, 1, 1, rows], partner, for_comb) for rows in halves]
    weight_outer, weight_edge = beside_weight[outer], beside_weight[edge]

    fill(0)
    came(w_in[1])
    go(w_on)
    pump(0)
    pass_on(0, 0)
    pump(1)
    came(w_in[0])
    came(w_on)
    spread()
    load_c.wait()
    load_own[0].wait()
    came(c_near)
    arrive(0, 0)
    left_side(0, parts[0], 0, 2)
    pump(2)
    left_side(0, parts[0], 2, 4)
    pump(3)
    acc[0] = right_side(parts[0], 0, 4)
    pump(4)
    pass_on(0, 1)
    pump(5)
    arrive(0, 1)
    left_side(0, parts[1], 0, 2)
    pump(6)
    left_side(0, parts[1], 2, 4)
    rest(0)
    acc[0] += right_side(parts[1], 0, 4)
    for copy in c_far:
        came(copy)
    left_side(0, full, 4, 6)
    rest(1)
    acc[0] += right_side(full, 4, 6)
    pass_on(1, 0)
    for copy in c_rest:
        came(copy)
    left_side(0, full, 6, 8)
    edge_own[...] = (acc[0] + right_side(full, 6, 8)).astype(BF16)
    go(to_across[0])
    go(to_beside[1])
    go(to_across[1])
    go(to_beside[0])

    fill(1)
    fill(2)
    for load in load_own[1:] + [load_r]:
        load.wait()
    rows = size // 4
    mine = pl.ds(pl.multiple_of(q * rows, rows), rows)
    here = y == 0
    for n, e in enumerate((core, 1 - core)):
        for m, s in enumerate((outer, edge)):
            real, imag = r_buf[e, s, 0, mine], r_buf[e, s, 1, mine]
            rows_of[n, m, 0] = jnp.concatenate([jnp.where(here, real, -imag), jnp.where(here, imag, real)], axis=0)
            rows_of[n, m, 1] = jnp.concatenate([jnp.where(here, -imag, real), jnp.where(here, real, imag)], axis=0)

    arrive(1, 0)
    left_side(1, parts[0], 0, 8)
    acc[1] = right_side(parts[0], 0, 8)
    pass_on(1, 1)
    arrive(1, 1)
    left_side(1, parts[1], 0, 8)
    total = acc[1] + right_side(parts[1], 0, 8)
    own = edge_own[...].astype(F32)
    comb[0, 0, 0] = (total + weight_outer * own).astype(BF16)
    go(to_partner[0, 0])
    acc[1] = own + weight_edge * total
    came(to_beside[1])
    came(to_across[0])
    for r in range(2):
        go(over_across[r])
        go(over_beside[r])
    pass_on(2, 0)
    arrive(2, 0)
    left_side(2, parts[0], 0, 8)
    acc[0] = right_side(parts[0], 0, 8)

    def project(n, m, c):
        return jnp.dot(rows_of[n, m, c], comb[n, m, c], preferred_element_type=F32)

    came(to_beside[0])
    comb[0, 1, 0] = (acc[1] + weight_edge * near_own[...].astype(F32)).astype(BF16)
    go(to_partner[1, 0])
    pass_on(2, 1)
    for n in range(2):
        for m in range(2):
            if n == 1:
                came(to_partner[m, 0])
            middle[n, m] = project(n, m, 0)
    came(to_across[1])
    arrive(2, 1)
    left_side(2, parts[1], 0, 8)
    acc[0] += right_side(parts[1], 0, 8)
    comb[0, 0, 1] = (acc[0] + weight_outer * edge_other[...].astype(F32)).astype(BF16)
    go(to_partner[0, 1])

    def finish(n):
        e = (core, 1 - core)[n]
        both = [(middle[n, m] + project(n, m, 1)).astype(BF16) for m in range(2)]
        for m, s in enumerate((outer, edge)):
            real, imag = both[m][:rows], both[m][rows:]
            sides = jnp.concatenate(
                [jnp.concatenate([real, imag], axis=1), jnp.concatenate([imag, -real], axis=1)], axis=0
            )
            updated = by_rows(sides, jnp.concatenate([r_buf[e, s, 0], r_buf[e, s, 1]], axis=1))
            out[e, s, 0] = updated[:rows]
            out[e, s, 1] = updated[rows:]

    def gather(r):
        came(over_across[r])
        came(over_beside[r])
        rows = halves[r]
        around = acc[0, rows] + near_other[rows].astype(F32)
        comb[0, 1, 1, rows] = (edge_other[rows].astype(F32) + weight_edge * around).astype(BF16)
        go(last_to_partner[r])

    gather(0)
    gather(1)
    finish(0)
    for copy in [to_partner[0, 1]] + last_to_partner:
        came(copy)
    finish(1)

    for n, (total, condition) in enumerate(groups):
        done = pltpu.make_async_remote_copy(
            src_ref=total, dst_ref=total, send_sem=send_sem.at[n], recv_sem=recv_sem.at[0],
            device_id=partner, device_id_type=MESH,
        )
        under(condition, done.wait_send)


def fast(lesser, retarded, coupling, occupations, offsets, intersection):
    nf, size, _ = coupling.shape
    rows = size // 4
    arrivals = 3 + 1 + 2 * len(RELAYS) + 2 + 4 + 6 * PIECES + 8 + 5
    anywhere = pl.BlockSpec(memory_space=pl.ANY)
    return pl.pallas_call(
        functools.partial(kernel, lax.axis_size("energy")),
        out_shape=pltpu.VMEM((2, 2, 2, rows, size), F32),
        in_specs=[anywhere] * 3 + [pl.BlockSpec(memory_space=pltpu.SMEM)] * 3,
        out_specs=pl.BlockSpec(memory_space=pltpu.VMEM),
        scratch_shapes=[
            pltpu.VMEM((PIECES, 4, size, size), BF16),
            pltpu.VMEM((4 * nf, size, size), BF16),
            pltpu.VMEM((4, 8, 128), F32),
            pltpu.VMEM((4 * nf, 4, 16, size), BF16),
            pltpu.VMEM((2, 2, 2, size, size), BF16),
            pltpu.VMEM((4 * nf, size, size), BF16),
            pltpu.VMEM((2, size, size), F32),
            pltpu.VMEM((size, size), BF16),
            pltpu.VMEM((size, size), BF16),
            pltpu.VMEM((size, size), BF16),
            pltpu.VMEM((size, size), BF16),
            pltpu.VMEM((2, 2, 2, size, size), BF16),
            pltpu.VMEM((2, 2, 2, 2 * rows, size), BF16),
            pltpu.VMEM((2, 2, 2 * rows, size), F32),
            pltpu.SemaphoreType.DMA((2 + PIECES,)),
            pltpu.SemaphoreType.DMA((GROUPS,)),
            pltpu.SemaphoreType.DMA((arrivals,)),
        ],
        compiler_params=pltpu.CompilerParams(
            collective_id=0, has_side_effects=True, vmem_limit_bytes=60 << 20
        ),
    )(lesser, retarded, coupling, occupations, offsets, intersection)


def solution(mesh):
    def shards(lesser, retarded, *rest):
        fits = (
            (mesh.shape["slab"], mesh.shape["freq"]) == (2, 4)
            and lesser.shape[:2] == (2, 2)
            and lesser.shape[-1] == 512
            and rest[0].shape[0] == 2
        )
        return (fast if fits else general)(lesser, retarded, *rest)

    return jax.shard_map(
        shards,
        mesh=mesh,
        in_specs=(
            P("energy", "slab", None, None, None),
            P("energy", "slab", None, None, None),
            P("freq", None, None),
            P("freq"),
            P("freq"),
            P("slab"),
        ),
        out_specs=P("energy", "slab", None, "freq", None),
        check_vma=False,
    )
```

```python
import functools
import jax
import jax.numpy as jnp
from jax import lax
from jax.experimental import pallas as pl
from jax.experimental.pallas import tpu as pltpu
from jax.sharding import PartitionSpec as P

OFFMAX = 2
UNROLL = 8
PIECES = 3
RELAYS = (96, 96, 64, 64, 64, 32)
SLIVER = 64
EARLY = 3
GROUPS = 16
MESH = pl.DeviceIdType.MESH
F32 = jnp.float32
BF16 = jnp.bfloat16


def with_halo(block, sides, width):
    for axis, dim in sides:
        count = lax.axis_size(axis)
        forward = [(i, i + 1) for i in range(count - 1)]
        backward = [(target, source) for source, target in forward]
        low = lax.ppermute(
            lax.slice_in_dim(block, block.shape[dim] - width, None, axis=dim), axis, forward
        )
        high = lax.ppermute(lax.slice_in_dim(block, 0, width, axis=dim), axis, backward)
        block = jnp.concatenate([low, block, high], axis=dim)
    return block


def general(lesser, retarded, coupling, occupations, offsets, intersection):
    freq_count = lax.axis_size("freq")
    row_count = lesser.shape[-1] // freq_count
    row_first = lax.axis_index("freq") * row_count
    padded = with_halo(lesser, (("energy", 0),), OFFMAX)
    energy_count = lesser.shape[0]
    positions = jnp.arange(energy_count, dtype=jnp.int32)[None, :] + OFFMAX
    lower_green = jnp.take(padded, positions - offsets[:, None], axis=0)
    upper_green = jnp.take(padded, positions + offsets[:, None], axis=0)
    scale = occupations[:, None, None, None, None, None]
    mixture = (
        scale * lower_green.astype(F32) + (scale + 1.0) * upper_green.astype(F32)
    ).astype(BF16)
    real_green = retarded[:, :, 0]
    imag_green = retarded[:, :, 1]
    real_rows = lax.dynamic_slice_in_dim(real_green, row_first, row_count, 2)
    imag_rows = lax.dynamic_slice_in_dim(imag_green, row_first, row_count, 2)
    left_product = jnp.einsum(
        "fri,fescij->fescrj", coupling, mixture, preferred_element_type=F32
    ).astype(BF16)
    self_energy = lax.psum_scatter(
        jnp.einsum(
            "fescrj,fkj->resck", left_product, coupling, preferred_element_type=F32
        ).astype(BF16),
        "freq",
        scatter_dimension=0,
        tiled=True,
    )
    beside_all = with_halo(self_energy, (("slab", 2),), 1)
    beside = beside_all[:, :, :-2].astype(F32) + beside_all[:, :, 2:].astype(F32)
    total = self_energy.astype(F32) + intersection[None, None, :, None, None] * beside
    combined = total.astype(BF16)
    real_self = combined[:, :, :, 0]
    imag_self = combined[:, :, :, 1]

    def by_transpose(left_side, right_side):
        return jnp.einsum("resj,eskj->resk", left_side, right_side, preferred_element_type=F32)

    real_part = by_transpose(real_self, real_green) + by_transpose(imag_self, imag_green)
    imag_part = by_transpose(imag_self, real_green) - by_transpose(real_self, imag_green)
    product = jnp.stack([real_part, imag_part], axis=3).astype(BF16)
    y_piece = lax.all_gather(product, "freq", axis=0, tiled=True)
    real_piece = y_piece[:, :, :, 0]
    imag_piece = y_piece[:, :, :, 1]

    def plain_product(left_side, right_side):
        return jnp.einsum("esrm,mesk->esrk", left_side, right_side, preferred_element_type=F32)

    out_real = plain_product(real_rows, real_piece) - plain_product(imag_rows, imag_piece)
    out_imag = plain_product(real_rows, imag_piece) + plain_product(imag_rows, real_piece)
    return jnp.stack([out_real, out_imag], axis=2)


def by_rows(a, b):
    return lax.dot_general(a, b, (((1,), (1,)), ((), ())), preferred_element_type=F32)


def kernel(
    energies,
    lesser, retarded, coupling, numbers, shifts, beside_weight, out,
    green, c_buf, w_tile, w_buf, r_buf, left_buf, acc, edge_own, edge_other, near_own, near_other,
    comb, rows_of, middle,
    local_sem, send_sem, recv_sem,
):
    nf, size, _ = coupling.shape
    half = size // 2
    x, q, z = lax.axis_index("slab"), lax.axis_index("freq"), lax.axis_index("energy")
    y, core = q // 2, q % 2
    outer, edge = x, 1 - x
    partner = {"freq": 2 * y + 1 - core}
    across = {"freq": 2 * (1 - y) + core}
    opposite = {"slab": 1 - x}
    has_low, has_high = z > 0, z < energies - 1
    first = core == 0
    second = core == 1
    has_to = jnp.logical_or(jnp.logical_and(first, has_high), jnp.logical_and(second, has_low))
    has_from = jnp.logical_or(jnp.logical_and(first, has_low), jnp.logical_and(second, has_high))
    along = {"energy": jnp.clip(z + 1 - 2 * core, 0, energies - 1)}
    behind = {"energy": jnp.clip(z - 1 + 2 * core, 0, energies - 1)}

    barrier = pltpu.get_barrier_semaphore()
    peers = [(None, partner), (None, across), (None, opposite), (has_from, behind)]

    def under(condition, action):
        if condition is None:
            action()
        else:
            pl.when(condition)(action)

    for condition, peer in peers:
        under(condition, lambda peer=peer: pl.semaphore_signal(barrier, inc=1, device_id=peer, device_id_type=MESH))

    count = [0]
    groups = []

    def group(total, condition=None):
        groups.append((total, condition))
        return len(groups) - 1, condition

    def remote(src, dst, peer, kind):
        n = count[0]
        count[0] += 1
        copy = pltpu.make_async_remote_copy(
            src_ref=src, dst_ref=dst, send_sem=send_sem.at[kind[0]], recv_sem=recv_sem.at[n],
            device_id=peer, device_id_type=MESH,
        )
        return copy, kind[1]

    def go(pair):
        under(pair[1], pair[0].start)
        return pair

    def came(pair):
        pair[0].wait_recv()

    pieces = [(edge, y), (outer, y), (outer, 1 - y)]
    near_slot, far_slot, own_slot = 2 * core, 2 * core + 1, 2 - 2 * core
    passed_slot, pass_to = 3 - 2 * core, 1 + 2 * core
    parts = [slice(0, half), slice(half, size)]
    load_c = pltpu.make_async_copy(coupling, c_buf.at[pl.ds(0, nf)], local_sem.at[0])
    load_r = pltpu.make_async_copy(retarded, r_buf, local_sem.at[1])
    load_own = [
        pltpu.make_async_copy(lesser.at[1 - core, s, c], green.at[p, own_slot], local_sem.at[2 + p])
        for p, (s, c) in enumerate(pieces)
    ]
    load_c.start()
    load_own[0].start()

    for i in range(nf):
        number, shift = numbers[i], shifts[i]
        none = jnp.float32(0.0)
        row = [
            jnp.where(shift == 1, number, none),
            jnp.where(shift == 2, number, none),
            jnp.where(shift == 1, number + 1.0, none),
            jnp.where(shift == 2, number + 1.0, none),
        ]
        for j in range(4):
            w_tile[0, 4 * i + j : 4 * i + j + 1, :] = jnp.full((1, 128), row[j], F32)

    def zero(p, slot):
        green[p, slot] = jnp.zeros((size, size), BF16)

    def fill(p):
        pl.when(jnp.logical_not(has_from))(lambda: zero(p, near_slot))
        pl.when(jnp.logical_not(has_from))(lambda: zero(p, far_slot))
        pl.when(jnp.logical_not(has_to))(lambda: zero(p, passed_slot))

    pl.semaphore_wait(barrier, 3 + has_to.astype(jnp.int32))

    starts = [sum(RELAYS[:b]) for b in range(len(RELAYS) + 1)]
    rows_at = [pl.ds(start, depth) for start, depth in zip(starts, RELAYS)]
    kept = pl.ds(starts[-1], size - starts[-1])
    staged = [pl.ds(0, starts[EARLY]), pl.ds(starts[EARLY], size - starts[EARLY])]
    for_w = group(w_tile.at[pl.ds(0, 3)])
    w_in = [go(remote(w_tile.at[0], w_tile.at[d + 1], peer, for_w)) for d, peer in enumerate((partner, across))]
    w_on = remote(w_tile.at[2], w_tile.at[3], partner, for_w)
    for_across = group(c_buf.at[4])
    for_direct = group(c_buf.at[4, kept])
    c_across = [go(remote(coupling.at[x, rows], c_buf.at[4, rows], across, for_across)) for rows in rows_at + [kept]]
    c_direct = go(remote(coupling.at[1 - x, kept], c_buf.at[6, kept], across, for_direct))
    sliver, most = pl.ds(size - SLIVER, SLIVER), pl.ds(0, size - SLIVER)
    for_z = group(green.at[pl.ds(0, 2), pl.ds(0, 2)], has_to)
    for_last = group(green.at[2, pl.ds(0, 2), most], has_to)
    for_passed = group(green.at[:, 0], has_from)
    for_side = group(green.at[1, pl.ds(0, 2), sliver], has_from)
    near, far, passed = {}, {}, {}
    for_near = group(coupling)

    def from_along(p, key, rows, columns, kind):
        s, c = pieces[p]
        near[p, key] = go(remote(lesser.at[1 - core, s, c, rows, columns], green.at[p, near_slot, rows, columns], along, kind))
        far[p, key] = go(remote(lesser.at[core, s, c, rows, columns], green.at[p, far_slot, rows, columns], along, kind))

    def to_pass(p, key, rows, columns):
        passed[p, key] = remote(green.at[p, near_slot, rows, columns], green.at[p, pass_to, rows, columns], partner, for_passed)

    every = pl.ds(0, size)
    for p in range(PIECES):
        if p == 1:
            from_along(1, 2, sliver, every, for_z)
            to_pass(1, 2, sliver, every)
        if p == 2:
            near[2, 2] = remote(green.at[1, near_slot, sliver], green.at[2, near_slot, sliver], across, for_side)
            far[2, 2] = remote(green.at[1, far_slot, sliver], green.at[2, far_slot, sliver], across, for_side)
            to_pass(2, 2, sliver, every)
        for k, columns in enumerate(parts):
            rows = every if p == 0 else most
            from_along(p, k, rows, columns, for_last if p == 2 else for_z)
            to_pass(p, k, rows, columns)
        if p == 0:
            c_near = go(remote(coupling, c_buf.at[pl.ds(nf, nf)], partner, for_near))
    for load in load_own[1:] + [load_r]:
        load.start()

    for_relay, for_far, for_rest = group(c_buf.at[4, pl.ds(0, starts[-1])]), group(c_buf.at[4]), group(c_buf.at[6])
    relayed = [remote(c_buf.at[4, rows], c_buf.at[6, rows], opposite, for_relay) for rows in rows_at]
    c_far = [remote(c_buf.at[4, rows], c_buf.at[5, rows], partner, for_far) for rows in staged]
    c_rest = [remote(c_buf.at[6, rows], c_buf.at[7, rows], partner, for_rest) for rows in staged]

    def pump(b):
        came(c_across[b])
        if b < len(relayed):
            go(relayed[b])
        if b == EARLY - 1:
            go(c_far[0])
        if b == len(relayed):
            go(c_far[1])

    def rest(h):
        for copy in (relayed[EARLY:] + [c_direct]) if h else relayed[:EARLY]:
            came(copy)
        go(c_rest[h])

    def pass_on(p, k):
        pl.when(has_from)(near[p, k][0].wait_recv)
        go(passed[p, k])

    def arrive(p, k):
        pl.when(has_from)(far[p, k][0].wait_recv)
        pl.when(has_to)(passed[p, k][0].wait_recv)

    def spread():
        for slot in range(4 * nf):
            source = slot // 2 if slot < 4 else 2 + slot % 2
            for i in range(4):
                if slot < 4:
                    row = w_tile[source, 4 * (slot % 2) + i : 4 * (slot % 2) + i + 1]
                else:
                    pair = (w_tile[source, i : i + 1], w_tile[source, 4 + i : 5 + i])
                    row = jnp.where((x == 0) == (slot < 6), pair[0], pair[1])
                wide = jnp.broadcast_to(row, (16, 128)).astype(BF16)
                w_buf[slot, i] = jnp.concatenate([wide] * (size // 128), axis=1)

    def mixture(p, columns, f):
        width = columns.stop - columns.start

        def term(i):
            block = green[p, i, :, columns].reshape(size // 16, 16, width)
            return w_buf[f, i, :, columns][None] * block

        return ((term(0) + term(1)) + (term(2) + term(3))).reshape(size, width)

    def left_side(p, columns, start, stop):
        def product(f, carry):
            left = jnp.dot(c_buf[f], mixture(p, columns, f), preferred_element_type=F32)
            left_buf[f, :, columns] = left.astype(BF16)
            return carry

        lax.fori_loop(start, stop, product, 0, unroll=min(UNROLL, stop - start))

    def right_side(columns, start, stop, rows=slice(None)):
        def beside(ref, rows):
            return jnp.concatenate([ref[f, rows, columns] for f in range(start, stop)], axis=1)

        return by_rows(beside(left_buf, rows), beside(c_buf, slice(None)))

    full = slice(0, size)
    halves = [pl.ds(h * half, half) for h in range(2)]
    for_edge, for_beside = group(edge_own), group(edge_own)
    to_across = [remote(edge_own.at[:, columns], edge_other.at[:, columns], across, for_edge) for columns in halves]
    to_beside = [remote(edge_own.at[:, columns], near_own.at[:, columns], opposite, for_beside) for columns in halves]
    for_over, for_under = group(near_own.at[:, halves[1]]), group(near_own.at[:, halves[1]])
    over_across = [remote(near_own.at[rows, halves[1]], near_other.at[rows, halves[1]], across, for_over) for rows in halves]
    over_beside = [remote(edge_other.at[rows, halves[0]], near_other.at[rows, halves[0]], opposite, for_under) for rows in halves]
    for_comb = group(comb.at[0])
    to_partner = [remote(comb.at[0, m, 0], comb.at[1, m, 0], partner, for_comb) for m in range(2)]
    late_to_partner = [remote(comb.at[0, 0, 1, rows], comb.at[1, 0, 1, rows], partner, for_comb) for rows in halves]
    last_to_partner = [remote(comb.at[0, 1, 1, rows], comb.at[1, 1, 1, rows], partner, for_comb) for rows in halves]
    weight_outer, weight_edge = beside_weight[outer], beside_weight[edge]

    fill(0)
    came(w_in[1])
    go(w_on)
    pump(0)
    pass_on(0, 0)
    pump(1)
    came(w_in[0])
    came(w_on)
    spread()
    load_c.wait()
    load_own[0].wait()
    came(c_near)
    arrive(0, 0)
    left_side(0, parts[0], 0, 2)
    pump(2)
    left_side(0, parts[0], 2, 4)
    pump(3)
    acc[0] = right_side(parts[0], 0, 4)
    pump(4)
    pass_on(0, 1)
    pump(5)
    arrive(0, 1)
    left_side(0, parts[1], 0, 2)
    pump(6)
    left_side(0, parts[1], 2, 4)
    rest(0)
    acc[0] += right_side(parts[1], 0, 4)
    pass_on(1, 2)
    pl.when(has_from)(far[1, 2][0].wait_recv)
    go(near[2, 2])
    go(far[2, 2])
    for copy in c_far:
        came(copy)
    left_side(0, full, 4, 6)
    rest(1)
    acc[0] += right_side(full, 4, 6)
    pass_on(1, 0)
    left_side(0, full, 6, 7)
    acc[0] += right_side(full, 6, 7)
    for copy in c_rest:
        came(copy)
    left_side(0, full, 7, 8)
    edge_own[...] = (acc[0] + right_side(full, 7, 8)).astype(BF16)
    go(to_across[0])
    go(to_beside[1])
    go(to_across[1])
    go(to_beside[0])

    fill(1)
    fill(2)
    for load in load_own[1:] + [load_r]:
        load.wait()
    rows = size // 4
    mine = pl.ds(pl.multiple_of(q * rows, rows), rows)
    here = y == 0
    for n, e in enumerate((core, 1 - core)):
        for m, s in enumerate((outer, edge)):
            real, imag = r_buf[e, s, 0, mine], r_buf[e, s, 1, mine]
            rows_of[n, m, 0] = jnp.concatenate([jnp.where(here, real, -imag), jnp.where(here, imag, real)], axis=0)
            rows_of[n, m, 1] = jnp.concatenate([jnp.where(here, -imag, real), jnp.where(here, real, imag)], axis=0)

    pass_on(2, 2)
    pl.when(has_to)(passed[1, 2][0].wait_recv)
    arrive(1, 0)
    left_side(1, parts[0], 0, 8)
    acc[1] = right_side(parts[0], 0, 8)
    pass_on(1, 1)
    arrive(1, 1)
    left_side(1, parts[1], 0, 8)
    total = acc[1] + right_side(parts[1], 0, 8)
    own = edge_own[...].astype(F32)
    comb[0, 0, 0] = (total + weight_outer * own).astype(BF16)
    go(to_partner[0])
    acc[1] = own + weight_edge * total
    came(to_beside[1])
    came(to_across[0])
    for r in range(2):
        go(over_across[r])
        go(over_beside[r])
    pass_on(2, 0)
    arrive(2, 2)
    arrive(2, 0)
    left_side(2, parts[0], 0, 8)
    acc[0] = right_side(parts[0], 0, 8)

    def project(n, m, c):
        return jnp.dot(rows_of[n, m, c], comb[n, m, c], preferred_element_type=F32)

    came(to_beside[0])
    comb[0, 1, 0] = (acc[1] + weight_edge * near_own[...].astype(F32)).astype(BF16)
    go(to_partner[1])
    pass_on(2, 1)
    for n in range(2):
        for m in range(2):
            if n == 1:
                came(to_partner[m])
            middle[n, m] = project(n, m, 0)
    came(to_across[1])
    arrive(2, 1)
    left_side(2, parts[1], 0, 8)
    for h, rows in enumerate(halves):
        acc[0, rows] += right_side(parts[1], 0, 8, rows)
        comb[0, 0, 1, rows] = (acc[0, rows] + weight_outer * edge_other[rows].astype(F32)).astype(BF16)
        go(late_to_partner[h])
    rows = size // 4

    def finish(*blocks):
        both = [(middle[n, m] + project(n, m, 1)).astype(BF16) for n, m in blocks]
        for (n, m), sums in zip(blocks, both):
            e, s = (core, 1 - core)[n], (outer, edge)[m]
            real, imag = sums[:rows], sums[rows:]
            sides = jnp.concatenate(
                [jnp.concatenate([real, imag], axis=1), jnp.concatenate([imag, -real], axis=1)], axis=0
            )
            updated = by_rows(sides, jnp.concatenate([r_buf[e, s, 0], r_buf[e, s, 1]], axis=1))
            out[e, s, 0] = updated[:rows]
            out[e, s, 1] = updated[rows:]

    def gather(r):
        came(over_across[r])
        came(over_beside[r])
        rows = halves[r]
        around = acc[0, rows] + near_other[rows].astype(F32)
        comb[0, 1, 1, rows] = (edge_other[rows].astype(F32) + weight_edge * around).astype(BF16)
        go(last_to_partner[r])

    gather(0)
    gather(1)
    finish((0, 0), (0, 1))
    for copy in late_to_partner:
        came(copy)
    finish((1, 0))
    for copy in last_to_partner:
        came(copy)
    finish((1, 1))

    for n, (total, condition) in enumerate(groups):
        done = pltpu.make_async_remote_copy(
            src_ref=total, dst_ref=total, send_sem=send_sem.at[n], recv_sem=recv_sem.at[0],
            device_id=partner, device_id_type=MESH,
        )
        under(condition, done.wait_send)


def fast(lesser, retarded, coupling, occupations, offsets, intersection):
    nf, size, _ = coupling.shape
    rows = size // 4
    arrivals = 3 + 1 + 2 * len(RELAYS) + 2 + 4 + 6 * PIECES + 6 + 8 + 6
    anywhere = pl.BlockSpec(memory_space=pl.ANY)
    return pl.pallas_call(
        functools.partial(kernel, lax.axis_size("energy")),
        out_shape=pltpu.VMEM((2, 2, 2, rows, size), F32),
        in_specs=[anywhere] * 3 + [pl.BlockSpec(memory_space=pltpu.SMEM)] * 3,
        out_specs=pl.BlockSpec(memory_space=pltpu.VMEM),
        scratch_shapes=[
            pltpu.VMEM((PIECES, 4, size, size), BF16),
            pltpu.VMEM((4 * nf, size, size), BF16),
            pltpu.VMEM((4, 8, 128), F32),
            pltpu.VMEM((4 * nf, 4, 16, size), BF16),
            pltpu.VMEM((2, 2, 2, size, size), BF16),
            pltpu.VMEM((4 * nf, size, size), BF16),
            pltpu.VMEM((2, size, size), F32),
            pltpu.VMEM((size, size), BF16),
            pltpu.VMEM((size, size), BF16),
            pltpu.VMEM((size, size), BF16),
            pltpu.VMEM((size, size), BF16),
            pltpu.VMEM((2, 2, 2, size, size), BF16),
            pltpu.VMEM((2, 2, 2, 2 * rows, size), BF16),
            pltpu.VMEM((2, 2, 2 * rows, size), F32),
            pltpu.SemaphoreType.DMA((2 + PIECES,)),
            pltpu.SemaphoreType.DMA((GROUPS,)),
            pltpu.SemaphoreType.DMA((arrivals,)),
        ],
        compiler_params=pltpu.CompilerParams(
            collective_id=0, has_side_effects=True, vmem_limit_bytes=60 << 20
        ),
    )(lesser, retarded, coupling, occupations, offsets, intersection)


def solution(mesh):
    def shards(lesser, retarded, *rest):
        fits = (
            (mesh.shape["slab"], mesh.shape["freq"]) == (2, 4)
            and lesser.shape[:2] == (2, 2)
            and lesser.shape[-1] == 512
            and rest[0].shape[0] == 2
        )
        return (fast if fits else general)(lesser, retarded, *rest)

    return jax.shard_map(
        shards,
        mesh=mesh,
        in_specs=(
            P("energy", "slab", None, None, None),
            P("energy", "slab", None, None, None),
            P("freq", None, None),
            P("freq"),
            P("freq"),
            P("slab"),
        ),
        out_specs=P("energy", "slab", None, "freq", None),
        check_vma=False,
    )
```

```python
import functools
import jax
import jax.numpy as jnp
from jax import lax
from jax.experimental import pallas as pl
from jax.experimental.pallas import tpu as pltpu
from jax.sharding import PartitionSpec as P

OFFMAX = 2
UNROLL = 8
PIECES = 3
RELAYS = (96, 96, 64, 64, 64, 48)
SLIVER = 64
EARLY = 3
GROUPS = 16
MESH = pl.DeviceIdType.MESH
F32 = jnp.float32
BF16 = jnp.bfloat16


def with_halo(block, sides, width):
    for axis, dim in sides:
        count = lax.axis_size(axis)
        forward = [(i, i + 1) for i in range(count - 1)]
        backward = [(target, source) for source, target in forward]
        low = lax.ppermute(
            lax.slice_in_dim(block, block.shape[dim] - width, None, axis=dim), axis, forward
        )
        high = lax.ppermute(lax.slice_in_dim(block, 0, width, axis=dim), axis, backward)
        block = jnp.concatenate([low, block, high], axis=dim)
    return block


def general(lesser, retarded, coupling, occupations, offsets, intersection):
    freq_count = lax.axis_size("freq")
    row_count = lesser.shape[-1] // freq_count
    row_first = lax.axis_index("freq") * row_count
    padded = with_halo(lesser, (("energy", 0),), OFFMAX)
    energy_count = lesser.shape[0]
    positions = jnp.arange(energy_count, dtype=jnp.int32)[None, :] + OFFMAX
    lower_green = jnp.take(padded, positions - offsets[:, None], axis=0)
    upper_green = jnp.take(padded, positions + offsets[:, None], axis=0)
    scale = occupations[:, None, None, None, None, None]
    mixture = (
        scale * lower_green.astype(F32) + (scale + 1.0) * upper_green.astype(F32)
    ).astype(BF16)
    real_green = retarded[:, :, 0]
    imag_green = retarded[:, :, 1]
    real_rows = lax.dynamic_slice_in_dim(real_green, row_first, row_count, 2)
    imag_rows = lax.dynamic_slice_in_dim(imag_green, row_first, row_count, 2)
    left_product = jnp.einsum(
        "fri,fescij->fescrj", coupling, mixture, preferred_element_type=F32
    ).astype(BF16)
    self_energy = lax.psum_scatter(
        jnp.einsum(
            "fescrj,fkj->resck", left_product, coupling, preferred_element_type=F32
        ).astype(BF16),
        "freq",
        scatter_dimension=0,
        tiled=True,
    )
    beside_all = with_halo(self_energy, (("slab", 2),), 1)
    beside = beside_all[:, :, :-2].astype(F32) + beside_all[:, :, 2:].astype(F32)
    total = self_energy.astype(F32) + intersection[None, None, :, None, None] * beside
    combined = total.astype(BF16)
    real_self = combined[:, :, :, 0]
    imag_self = combined[:, :, :, 1]

    def by_transpose(left_side, right_side):
        return jnp.einsum("resj,eskj->resk", left_side, right_side, preferred_element_type=F32)

    real_part = by_transpose(real_self, real_green) + by_transpose(imag_self, imag_green)
    imag_part = by_transpose(imag_self, real_green) - by_transpose(real_self, imag_green)
    product = jnp.stack([real_part, imag_part], axis=3).astype(BF16)
    y_piece = lax.all_gather(product, "freq", axis=0, tiled=True)
    real_piece = y_piece[:, :, :, 0]
    imag_piece = y_piece[:, :, :, 1]

    def plain_product(left_side, right_side):
        return jnp.einsum("esrm,mesk->esrk", left_side, right_side, preferred_element_type=F32)

    out_real = plain_product(real_rows, real_piece) - plain_product(imag_rows, imag_piece)
    out_imag = plain_product(real_rows, imag_piece) + plain_product(imag_rows, real_piece)
    return jnp.stack([out_real, out_imag], axis=2)


def by_rows(a, b):
    return lax.dot_general(a, b, (((1,), (1,)), ((), ())), preferred_element_type=F32)


def kernel(
    energies,
    lesser, retarded, coupling, numbers, shifts, beside_weight, out,
    green, c_buf, w_tile, w_buf, r_buf, left_buf, acc, edge_own, edge_other, near_own, near_other,
    comb, rows_of, middle,
    local_sem, send_sem, recv_sem,
):
    nf, size, _ = coupling.shape
    half = size // 2
    x, q, z = lax.axis_index("slab"), lax.axis_index("freq"), lax.axis_index("energy")
    y, core = q // 2, q % 2
    outer, edge = x, 1 - x
    partner = {"freq": 2 * y + 1 - core}
    across = {"freq": 2 * (1 - y) + core}
    opposite = {"slab": 1 - x}
    has_low, has_high = z > 0, z < energies - 1
    first = core == 0
    second = core == 1
    has_to = jnp.logical_or(jnp.logical_and(first, has_high), jnp.logical_and(second, has_low))
    has_from = jnp.logical_or(jnp.logical_and(first, has_low), jnp.logical_and(second, has_high))
    along = {"energy": jnp.clip(z + 1 - 2 * core, 0, energies - 1)}
    behind = {"energy": jnp.clip(z - 1 + 2 * core, 0, energies - 1)}

    barrier = pltpu.get_barrier_semaphore()
    peers = [(None, partner), (None, across), (None, opposite), (has_from, behind)]

    def under(condition, action):
        if condition is None:
            action()
        else:
            pl.when(condition)(action)

    for condition, peer in peers:
        under(condition, lambda peer=peer: pl.semaphore_signal(barrier, inc=1, device_id=peer, device_id_type=MESH))

    count = [0]
    groups = []

    def group(total, condition=None):
        groups.append((total, condition))
        return len(groups) - 1, condition

    def remote(src, dst, peer, kind):
        n = count[0]
        count[0] += 1
        copy = pltpu.make_async_remote_copy(
            src_ref=src, dst_ref=dst, send_sem=send_sem.at[kind[0]], recv_sem=recv_sem.at[n],
            device_id=peer, device_id_type=MESH,
        )
        return copy, kind[1]

    def go(pair):
        under(pair[1], pair[0].start)
        return pair

    def came(pair):
        pair[0].wait_recv()

    pieces = [(edge, y), (outer, y), (outer, 1 - y)]
    near_slot, far_slot, own_slot = 2 * core, 2 * core + 1, 2 - 2 * core
    passed_slot, pass_to = 3 - 2 * core, 1 + 2 * core
    parts = [slice(0, half), slice(half, size)]
    load_c = pltpu.make_async_copy(coupling, c_buf.at[pl.ds(0, nf)], local_sem.at[0])
    load_r = pltpu.make_async_copy(retarded, r_buf, local_sem.at[1])
    load_own = [
        pltpu.make_async_copy(lesser.at[1 - core, s, c], green.at[p, own_slot], local_sem.at[2 + p])
        for p, (s, c) in enumerate(pieces)
    ]
    load_c.start()
    load_own[0].start()

    for i in range(nf):
        number, shift = numbers[i], shifts[i]
        none = jnp.float32(0.0)
        row = [
            jnp.where(shift == 1, number, none),
            jnp.where(shift == 2, number, none),
            jnp.where(shift == 1, number + 1.0, none),
            jnp.where(shift == 2, number + 1.0, none),
        ]
        for j in range(4):
            w_tile[0, 4 * i + j : 4 * i + j + 1, :] = jnp.full((1, 128), row[j], F32)

    def zero(p, slot):
        green[p, slot] = jnp.zeros((size, size), BF16)

    def fill(p):
        pl.when(jnp.logical_not(has_from))(lambda: zero(p, near_slot))
        pl.when(jnp.logical_not(has_from))(lambda: zero(p, far_slot))
        pl.when(jnp.logical_not(has_to))(lambda: zero(p, passed_slot))

    pl.semaphore_wait(barrier, 3 + has_to.astype(jnp.int32))

    starts = [sum(RELAYS[:b]) for b in range(len(RELAYS) + 1)]
    rows_at = [pl.ds(start, depth) for start, depth in zip(starts, RELAYS)]
    kept = pl.ds(starts[-1], size - starts[-1])
    staged = [pl.ds(0, starts[EARLY]), pl.ds(starts[EARLY], size - starts[EARLY])]
    for_w = group(w_tile.at[pl.ds(0, 3)])
    w_in = [go(remote(w_tile.at[0], w_tile.at[d + 1], peer, for_w)) for d, peer in enumerate((partner, across))]
    w_on = remote(w_tile.at[2], w_tile.at[3], partner, for_w)
    for_across = group(c_buf.at[4])
    for_direct = group(c_buf.at[4, kept])
    c_across = [go(remote(coupling.at[x, rows], c_buf.at[4, rows], across, for_across)) for rows in rows_at + [kept]]
    c_direct = go(remote(coupling.at[1 - x, kept], c_buf.at[6, kept], across, for_direct))
    sliver, most = pl.ds(size - SLIVER, SLIVER), pl.ds(0, size - SLIVER)
    for_z = group(green.at[pl.ds(0, 2), pl.ds(0, 2)], has_to)
    for_last = group(green.at[2, pl.ds(0, 2), most], has_to)
    for_passed = group(green.at[:, 0], has_from)
    for_side = group(green.at[1, pl.ds(0, 2), sliver], has_from)
    near, far, passed = {}, {}, {}
    for_near = group(coupling)

    def from_along(p, key, rows, columns, kind):
        s, c = pieces[p]
        near[p, key] = go(remote(lesser.at[1 - core, s, c, rows, columns], green.at[p, near_slot, rows, columns], along, kind))
        far[p, key] = go(remote(lesser.at[core, s, c, rows, columns], green.at[p, far_slot, rows, columns], along, kind))

    def to_pass(p, key, rows, columns):
        passed[p, key] = remote(green.at[p, near_slot, rows, columns], green.at[p, pass_to, rows, columns], partner, for_passed)

    every = pl.ds(0, size)
    for p in range(PIECES):
        if p == 1:
            from_along(1, 2, sliver, every, for_z)
            to_pass(1, 2, sliver, every)
        if p == 2:
            near[2, 2] = remote(green.at[1, near_slot, sliver], green.at[2, near_slot, sliver], across, for_side)
            far[2, 2] = remote(green.at[1, far_slot, sliver], green.at[2, far_slot, sliver], across, for_side)
            to_pass(2, 2, sliver, every)
        for k, columns in enumerate(parts):
            rows = every if p == 0 else most
            from_along(p, k, rows, columns, for_last if p == 2 else for_z)
            to_pass(p, k, rows, columns)
        if p == 0:
            c_near = go(remote(coupling, c_buf.at[pl.ds(nf, nf)], partner, for_near))
    for load in load_own[1:] + [load_r]:
        load.start()

    for_relay, for_far, for_rest = group(c_buf.at[4, pl.ds(0, starts[-1])]), group(c_buf.at[4]), group(c_buf.at[6])
    relayed = [remote(c_buf.at[4, rows], c_buf.at[6, rows], opposite, for_relay) for rows in rows_at]
    c_far = [remote(c_buf.at[4, rows], c_buf.at[5, rows], partner, for_far) for rows in staged]
    c_rest = [remote(c_buf.at[6, rows], c_buf.at[7, rows], partner, for_rest) for rows in staged]

    def pump(b):
        came(c_across[b])
        if b < len(relayed):
            go(relayed[b])
        if b == EARLY - 1:
            go(c_far[0])
        if b == len(relayed):
            go(c_far[1])

    def rest(h):
        for copy in (relayed[EARLY:] + [c_direct]) if h else relayed[:EARLY]:
            came(copy)
        go(c_rest[h])

    def pass_on(p, k):
        pl.when(has_from)(near[p, k][0].wait_recv)
        go(passed[p, k])

    def arrive(p, k):
        pl.when(has_from)(far[p, k][0].wait_recv)
        pl.when(has_to)(passed[p, k][0].wait_recv)

    def spread():
        for slot in range(4 * nf):
            source = slot // 2 if slot < 4 else 2 + slot % 2
            for i in range(4):
                if slot < 4:
                    row = w_tile[source, 4 * (slot % 2) + i : 4 * (slot % 2) + i + 1]
                else:
                    pair = (w_tile[source, i : i + 1], w_tile[source, 4 + i : 5 + i])
                    row = jnp.where((x == 0) == (slot < 6), pair[0], pair[1])
                wide = jnp.broadcast_to(row, (16, 128)).astype(BF16)
                w_buf[slot, i] = jnp.concatenate([wide] * (size // 128), axis=1)

    def mixture(p, columns, f):
        width = columns.stop - columns.start

        def term(i):
            block = green[p, i, :, columns].reshape(size // 16, 16, width)
            return w_buf[f, i, :, columns][None] * block

        return ((term(0) + term(1)) + (term(2) + term(3))).reshape(size, width)

    def left_side(p, columns, start, stop):
        def product(f, carry):
            left = jnp.dot(c_buf[f], mixture(p, columns, f), preferred_element_type=F32)
            left_buf[f, :, columns] = left.astype(BF16)
            return carry

        lax.fori_loop(start, stop, product, 0, unroll=min(UNROLL, stop - start))

    def right_side(columns, start, stop, rows=slice(None)):
        def beside(ref, rows):
            return jnp.concatenate([ref[f, rows, columns] for f in range(start, stop)], axis=1)

        return by_rows(beside(left_buf, rows), beside(c_buf, slice(None)))

    full = slice(0, size)
    halves = [pl.ds(h * half, half) for h in range(2)]
    for_edge, for_beside = group(edge_own), group(edge_own)
    to_across = [remote(edge_own.at[:, columns], edge_other.at[:, columns], across, for_edge) for columns in halves]
    to_beside = [remote(edge_own.at[:, columns], near_own.at[:, columns], opposite, for_beside) for columns in halves]
    for_over, for_under = group(near_own.at[:, halves[1]]), group(near_own.at[:, halves[1]])
    uneven = [pl.ds(0, size - size // 4), pl.ds(size - size // 4, size // 4)]
    over_across = [remote(near_own.at[rows, halves[1]], near_other.at[rows, halves[1]], across, for_over) for rows in uneven]
    over_beside = [remote(edge_other.at[rows, halves[0]], near_other.at[rows, halves[0]], opposite, for_under) for rows in uneven]
    for_comb = group(comb.at[0])
    to_partner = [remote(comb.at[0, m, 0], comb.at[1, m, 0], partner, for_comb) for m in range(2)]
    late_to_partner = [remote(comb.at[0, 0, 1, rows], comb.at[1, 0, 1, rows], partner, for_comb) for rows in halves]
    last_to_partner = [remote(comb.at[0, 1, 1, rows], comb.at[1, 1, 1, rows], partner, for_comb) for rows in uneven]
    weight_outer, weight_edge = beside_weight[outer], beside_weight[edge]

    fill(0)
    came(w_in[1])
    go(w_on)
    pump(0)
    pass_on(0, 0)
    pump(1)
    came(w_in[0])
    came(w_on)
    spread()
    load_c.wait()
    load_own[0].wait()
    came(c_near)
    arrive(0, 0)
    left_side(0, parts[0], 0, 2)
    pump(2)
    left_side(0, parts[0], 2, 4)
    pump(3)
    acc[0] = right_side(parts[0], 0, 4)
    pump(4)
    pass_on(0, 1)
    pump(5)
    arrive(0, 1)
    left_side(0, parts[1], 0, 2)
    pump(6)
    left_side(0, parts[1], 2, 4)
    rest(0)
    acc[0] += right_side(parts[1], 0, 4)
    pass_on(1, 2)
    pl.when(has_from)(far[1, 2][0].wait_recv)
    go(near[2, 2])
    go(far[2, 2])
    for copy in c_far:
        came(copy)
    left_side(0, full, 4, 6)
    rest(1)
    acc[0] += right_side(full, 4, 6)
    pass_on(1, 0)
    left_side(0, full, 6, 7)
    acc[0] += right_side(full, 6, 7)
    for copy in c_rest:
        came(copy)
    left_side(0, full, 7, 8)
    edge_own[...] = (acc[0] + right_side(full, 7, 8)).astype(BF16)
    go(to_across[0])
    go(to_beside[1])
    go(to_across[1])
    go(to_beside[0])

    fill(1)
    fill(2)
    for load in load_own[1:] + [load_r]:
        load.wait()
    rows = size // 4
    mine = pl.ds(pl.multiple_of(q * rows, rows), rows)
    here = y == 0
    for n, e in enumerate((core, 1 - core)):
        for m, s in enumerate((outer, edge)):
            real, imag = r_buf[e, s, 0, mine], r_buf[e, s, 1, mine]
            rows_of[n, m, 0] = jnp.concatenate([jnp.where(here, real, -imag), jnp.where(here, imag, real)], axis=0)
            rows_of[n, m, 1] = jnp.concatenate([jnp.where(here, -imag, real), jnp.where(here, real, imag)], axis=0)

    pass_on(2, 2)
    pl.when(has_to)(passed[1, 2][0].wait_recv)
    arrive(1, 0)
    left_side(1, parts[0], 0, 8)
    acc[1] = right_side(parts[0], 0, 8)
    pass_on(1, 1)
    arrive(1, 1)
    left_side(1, parts[1], 0, 8)
    total = acc[1] + right_side(parts[1], 0, 8)
    own = edge_own[...].astype(F32)
    comb[0, 0, 0] = (total + weight_outer * own).astype(BF16)
    go(to_partner[0])
    acc[1] = own + weight_edge * total
    came(to_beside[1])
    came(to_across[0])
    for r in range(2):
        go(over_across[r])
        go(over_beside[r])
    pass_on(2, 0)
    arrive(2, 2)
    arrive(2, 0)
    left_side(2, parts[0], 0, 8)
    acc[0] = right_side(parts[0], 0, 8)

    def project(n, m, c):
        return jnp.dot(rows_of[n, m, c], comb[n, m, c], preferred_element_type=F32)

    came(to_beside[0])
    comb[0, 1, 0] = (acc[1] + weight_edge * near_own[...].astype(F32)).astype(BF16)
    go(to_partner[1])
    pass_on(2, 1)
    for n in range(2):
        for m in range(2):
            if n == 1:
                came(to_partner[m])
            middle[n, m] = project(n, m, 0)
    came(to_across[1])
    arrive(2, 1)
    left_side(2, parts[1], 0, 8)
    for h, rows in enumerate(halves):
        acc[0, rows] += right_side(parts[1], 0, 8, rows)
        comb[0, 0, 1, rows] = (acc[0, rows] + weight_outer * edge_other[rows].astype(F32)).astype(BF16)
        go(late_to_partner[h])
    rows = size // 4

    def finish(*blocks):
        both = [(middle[n, m] + project(n, m, 1)).astype(BF16) for n, m in blocks]
        for (n, m), sums in zip(blocks, both):
            e, s = (core, 1 - core)[n], (outer, edge)[m]
            real, imag = sums[:rows], sums[rows:]
            sides = jnp.concatenate(
                [jnp.concatenate([real, imag], axis=1), jnp.concatenate([imag, -real], axis=1)], axis=0
            )
            updated = by_rows(sides, jnp.concatenate([r_buf[e, s, 0], r_buf[e, s, 1]], axis=1))
            out[e, s, 0] = updated[:rows]
            out[e, s, 1] = updated[rows:]

    def gather(r):
        came(over_across[r])
        came(over_beside[r])
        rows = uneven[r]
        around = acc[0, rows] + near_other[rows].astype(F32)
        comb[0, 1, 1, rows] = (edge_other[rows].astype(F32) + weight_edge * around).astype(BF16)
        go(last_to_partner[r])

    gather(0)
    finish((0, 0))
    gather(1)
    for copy in late_to_partner:
        came(copy)
    finish((0, 1), (1, 0))
    for copy in last_to_partner:
        came(copy)
    finish((1, 1))

    for n, (total, condition) in enumerate(groups):
        done = pltpu.make_async_remote_copy(
            src_ref=total, dst_ref=total, send_sem=send_sem.at[n], recv_sem=recv_sem.at[0],
            device_id=partner, device_id_type=MESH,
        )
        under(condition, done.wait_send)


def fast(lesser, retarded, coupling, occupations, offsets, intersection):
    nf, size, _ = coupling.shape
    rows = size // 4
    arrivals = 3 + 1 + 2 * len(RELAYS) + 2 + 4 + 6 * PIECES + 6 + 8 + 6
    anywhere = pl.BlockSpec(memory_space=pl.ANY)
    return pl.pallas_call(
        functools.partial(kernel, lax.axis_size("energy")),
        out_shape=pltpu.VMEM((2, 2, 2, rows, size), F32),
        in_specs=[anywhere] * 3 + [pl.BlockSpec(memory_space=pltpu.SMEM)] * 3,
        out_specs=pl.BlockSpec(memory_space=pltpu.VMEM),
        scratch_shapes=[
            pltpu.VMEM((PIECES, 4, size, size), BF16),
            pltpu.VMEM((4 * nf, size, size), BF16),
            pltpu.VMEM((4, 8, 128), F32),
            pltpu.VMEM((4 * nf, 4, 16, size), BF16),
            pltpu.VMEM((2, 2, 2, size, size), BF16),
            pltpu.VMEM((4 * nf, size, size), BF16),
            pltpu.VMEM((2, size, size), F32),
            pltpu.VMEM((size, size), BF16),
            pltpu.VMEM((size, size), BF16),
            pltpu.VMEM((size, size), BF16),
            pltpu.VMEM((size, size), BF16),
            pltpu.VMEM((2, 2, 2, size, size), BF16),
            pltpu.VMEM((2, 2, 2, 2 * rows, size), BF16),
            pltpu.VMEM((2, 2, 2 * rows, size), F32),
            pltpu.SemaphoreType.DMA((2 + PIECES,)),
            pltpu.SemaphoreType.DMA((GROUPS,)),
            pltpu.SemaphoreType.DMA((arrivals,)),
        ],
        compiler_params=pltpu.CompilerParams(
            collective_id=0, has_side_effects=True, vmem_limit_bytes=60 << 20
        ),
    )(lesser, retarded, coupling, occupations, offsets, intersection)


def solution(mesh):
    def shards(lesser, retarded, *rest):
        fits = (
            (mesh.shape["slab"], mesh.shape["freq"]) == (2, 4)
            and lesser.shape[:2] == (2, 2)
            and lesser.shape[-1] == 512
            and rest[0].shape[0] == 2
        )
        return (fast if fits else general)(lesser, retarded, *rest)

    return jax.shard_map(
        shards,
        mesh=mesh,
        in_specs=(
            P("energy", "slab", None, None, None),
            P("energy", "slab", None, None, None),
            P("freq", None, None),
            P("freq"),
            P("freq"),
            P("slab"),
        ),
        out_specs=P("energy", "slab", None, "freq", None),
        check_vma=False,
    )
```

```python
import functools
import jax
import jax.numpy as jnp
from jax import lax
from jax.experimental import pallas as pl
from jax.experimental.pallas import tpu as pltpu
from jax.sharding import PartitionSpec as P

OFFMAX = 2
UNROLL = 8
PIECES = 3
RELAYS = (96, 96, 64, 64, 64, 48)
SLIVER = 64
EARLY = 3
GROUPS = 8
MESH = pl.DeviceIdType.MESH
F32 = jnp.float32
BF16 = jnp.bfloat16


def with_halo(block, sides, width):
    for axis, dim in sides:
        count = lax.axis_size(axis)
        forward = [(i, i + 1) for i in range(count - 1)]
        backward = [(target, source) for source, target in forward]
        low = lax.ppermute(
            lax.slice_in_dim(block, block.shape[dim] - width, None, axis=dim), axis, forward
        )
        high = lax.ppermute(lax.slice_in_dim(block, 0, width, axis=dim), axis, backward)
        block = jnp.concatenate([low, block, high], axis=dim)
    return block


def general(lesser, retarded, coupling, occupations, offsets, intersection):
    freq_count = lax.axis_size("freq")
    row_count = lesser.shape[-1] // freq_count
    row_first = lax.axis_index("freq") * row_count
    padded = with_halo(lesser, (("energy", 0),), OFFMAX)
    energy_count = lesser.shape[0]
    positions = jnp.arange(energy_count, dtype=jnp.int32)[None, :] + OFFMAX
    lower_green = jnp.take(padded, positions - offsets[:, None], axis=0)
    upper_green = jnp.take(padded, positions + offsets[:, None], axis=0)
    scale = occupations[:, None, None, None, None, None]
    mixture = (
        scale * lower_green.astype(F32) + (scale + 1.0) * upper_green.astype(F32)
    ).astype(BF16)
    real_green = retarded[:, :, 0]
    imag_green = retarded[:, :, 1]
    real_rows = lax.dynamic_slice_in_dim(real_green, row_first, row_count, 2)
    imag_rows = lax.dynamic_slice_in_dim(imag_green, row_first, row_count, 2)
    left_product = jnp.einsum(
        "fri,fescij->fescrj", coupling, mixture, preferred_element_type=F32
    ).astype(BF16)
    self_energy = lax.psum_scatter(
        jnp.einsum(
            "fescrj,fkj->resck", left_product, coupling, preferred_element_type=F32
        ).astype(BF16),
        "freq",
        scatter_dimension=0,
        tiled=True,
    )
    beside_all = with_halo(self_energy, (("slab", 2),), 1)
    beside = beside_all[:, :, :-2].astype(F32) + beside_all[:, :, 2:].astype(F32)
    total = self_energy.astype(F32) + intersection[None, None, :, None, None] * beside
    combined = total.astype(BF16)
    real_self = combined[:, :, :, 0]
    imag_self = combined[:, :, :, 1]

    def by_transpose(left_side, right_side):
        return jnp.einsum("resj,eskj->resk", left_side, right_side, preferred_element_type=F32)

    real_part = by_transpose(real_self, real_green) + by_transpose(imag_self, imag_green)
    imag_part = by_transpose(imag_self, real_green) - by_transpose(real_self, imag_green)
    product = jnp.stack([real_part, imag_part], axis=3).astype(BF16)
    y_piece = lax.all_gather(product, "freq", axis=0, tiled=True)
    real_piece = y_piece[:, :, :, 0]
    imag_piece = y_piece[:, :, :, 1]

    def plain_product(left_side, right_side):
        return jnp.einsum("esrm,mesk->esrk", left_side, right_side, preferred_element_type=F32)

    out_real = plain_product(real_rows, real_piece) - plain_product(imag_rows, imag_piece)
    out_imag = plain_product(real_rows, imag_piece) + plain_product(imag_rows, real_piece)
    return jnp.stack([out_real, out_imag], axis=2)


def by_rows(a, b):
    return lax.dot_general(a, b, (((1,), (1,)), ((), ())), preferred_element_type=F32)


def kernel(
    energies,
    lesser, retarded, coupling, numbers, shifts, beside_weight, out,
    green, c_buf, w_tile, w_buf, r_buf, left_buf, acc, edge_own, edge_other, near_own, near_other,
    comb, rows_of, middle,
    local_sem, send_sem, recv_sem,
):
    nf, size, _ = coupling.shape
    half = size // 2
    x, q, z = lax.axis_index("slab"), lax.axis_index("freq"), lax.axis_index("energy")
    y, core = q // 2, q % 2
    outer, edge = x, 1 - x
    partner = {"freq": 2 * y + 1 - core}
    across = {"freq": 2 * (1 - y) + core}
    opposite = {"slab": 1 - x}
    has_low, has_high = z > 0, z < energies - 1
    first = core == 0
    second = core == 1
    has_to = jnp.logical_or(jnp.logical_and(first, has_high), jnp.logical_and(second, has_low))
    has_from = jnp.logical_or(jnp.logical_and(first, has_low), jnp.logical_and(second, has_high))
    along = {"energy": jnp.clip(z + 1 - 2 * core, 0, energies - 1)}
    behind = {"energy": jnp.clip(z - 1 + 2 * core, 0, energies - 1)}

    barrier = pltpu.get_barrier_semaphore()
    peers = [(None, partner), (None, across), (None, opposite), (has_from, behind)]

    def under(condition, action):
        if condition is None:
            action()
        else:
            pl.when(condition)(action)

    for condition, peer in peers:
        under(condition, lambda peer=peer: pl.semaphore_signal(barrier, inc=1, device_id=peer, device_id_type=MESH))

    count = [0]
    groups = []

    def group(total, condition=None):
        groups.append((total, condition))
        return len(groups) - 1, condition

    def remote(src, dst, peer, kind):
        n = count[0]
        count[0] += 1
        copy = pltpu.make_async_remote_copy(
            src_ref=src, dst_ref=dst, send_sem=send_sem.at[kind[0]], recv_sem=recv_sem.at[n],
            device_id=peer, device_id_type=MESH,
        )
        return copy, kind[1]

    def go(pair):
        under(pair[1], pair[0].start)
        return pair

    def came(pair):
        pair[0].wait_recv()

    pieces = [(edge, y), (outer, y), (outer, 1 - y)]
    near_slot, far_slot, own_slot = 2 * core, 2 * core + 1, 2 - 2 * core
    passed_slot, pass_to = 3 - 2 * core, 1 + 2 * core
    parts = [slice(0, half), slice(half, size)]
    load_c = pltpu.make_async_copy(coupling, c_buf.at[pl.ds(0, nf)], local_sem.at[0])
    load_r = pltpu.make_async_copy(retarded, r_buf, local_sem.at[1])
    load_own = [
        pltpu.make_async_copy(lesser.at[1 - core, s, c], green.at[p, own_slot], local_sem.at[2 + p])
        for p, (s, c) in enumerate(pieces)
    ]
    load_c.start()
    load_own[0].start()

    for i in range(nf):
        number, shift = numbers[i], shifts[i]
        none = jnp.float32(0.0)
        row = [
            jnp.where(shift == 1, number, none),
            jnp.where(shift == 2, number, none),
            jnp.where(shift == 1, number + 1.0, none),
            jnp.where(shift == 2, number + 1.0, none),
        ]
        for j in range(4):
            w_tile[0, 4 * i + j : 4 * i + j + 1, :] = jnp.full((1, 128), row[j], F32)

    def zero(p, slot):
        green[p, slot] = jnp.zeros((size, size), BF16)

    def fill(p):
        pl.when(jnp.logical_not(has_from))(lambda: zero(p, near_slot))
        pl.when(jnp.logical_not(has_from))(lambda: zero(p, far_slot))
        pl.when(jnp.logical_not(has_to))(lambda: zero(p, passed_slot))

    pl.semaphore_wait(barrier, 3 + has_to.astype(jnp.int32))

    starts = [sum(RELAYS[:b]) for b in range(len(RELAYS) + 1)]
    rows_at = [pl.ds(start, depth) for start, depth in zip(starts, RELAYS)]
    kept = pl.ds(starts[-1], size - starts[-1])
    staged = [pl.ds(0, starts[EARLY]), pl.ds(starts[EARLY], size - starts[EARLY])]
    for_w = group(w_tile.at[pl.ds(0, 3)])
    w_in = [go(remote(w_tile.at[0], w_tile.at[d + 1], peer, for_w)) for d, peer in enumerate((partner, across))]
    w_on = remote(w_tile.at[2], w_tile.at[3], partner, for_w)
    for_blocks = for_across = for_direct = group(green.at[0])
    for_sums = group(c_buf)
    c_across = [go(remote(coupling.at[x, rows], c_buf.at[4, rows], across, for_across)) for rows in rows_at + [kept]]
    c_direct = go(remote(coupling.at[1 - x, kept], c_buf.at[6, kept], across, for_direct))
    sliver, most = pl.ds(size - SLIVER, SLIVER), pl.ds(0, size - SLIVER)
    for_z = group(green.at[pl.ds(0, 2), pl.ds(0, 2)], has_to)
    for_last = group(green.at[2, pl.ds(0, 2), most], has_to)
    for_passed = group(green.at[:, 0], has_from)
    for_side = group(green.at[1, pl.ds(0, 2), sliver], has_from)
    near, far, passed = {}, {}, {}
    for_near = for_sums

    def from_along(p, key, rows, columns, kind):
        s, c = pieces[p]
        near[p, key] = go(remote(lesser.at[1 - core, s, c, rows, columns], green.at[p, near_slot, rows, columns], along, kind))
        far[p, key] = go(remote(lesser.at[core, s, c, rows, columns], green.at[p, far_slot, rows, columns], along, kind))

    def to_pass(p, key, rows, columns):
        passed[p, key] = remote(green.at[p, near_slot, rows, columns], green.at[p, pass_to, rows, columns], partner, for_passed)

    every = pl.ds(0, size)
    for p in range(PIECES):
        if p == 1:
            from_along(1, 2, sliver, every, for_z)
            to_pass(1, 2, sliver, every)
        if p == 2:
            near[2, 2] = remote(green.at[1, near_slot, sliver], green.at[2, near_slot, sliver], across, for_side)
            far[2, 2] = remote(green.at[1, far_slot, sliver], green.at[2, far_slot, sliver], across, for_side)
            to_pass(2, 2, sliver, every)
        for k, columns in enumerate(parts):
            rows = every if p == 0 else most
            from_along(p, k, rows, columns, for_last if p == 2 else for_z)
            to_pass(p, k, rows, columns)
        if p == 0:
            c_near = go(remote(coupling, c_buf.at[pl.ds(nf, nf)], partner, for_near))
    for load in load_own[1:] + [load_r]:
        load.start()

    for_relay = for_far = for_rest = for_blocks
    relayed = [remote(c_buf.at[4, rows], c_buf.at[6, rows], opposite, for_relay) for rows in rows_at]
    c_far = [remote(c_buf.at[4, rows], c_buf.at[5, rows], partner, for_far) for rows in staged]
    stages = [staged[0], pl.ds(starts[EARLY], starts[-1] - starts[EARLY]), kept]
    c_rest = [remote(c_buf.at[6, rows], c_buf.at[7, rows], partner, for_rest) for rows in stages]

    def pump(b):
        came(c_across[b])
        if b < len(relayed):
            go(relayed[b])
        if b == EARLY - 1:
            go(c_far[0])
        if b == len(relayed):
            go(c_far[1])

    def rest(h):
        for copy in (relayed[:EARLY], relayed[EARLY:], [c_direct])[h]:
            came(copy)
        go(c_rest[h])

    def pass_on(p, k):
        pl.when(has_from)(near[p, k][0].wait_recv)
        go(passed[p, k])

    def arrive(p, k):
        pl.when(has_from)(far[p, k][0].wait_recv)
        pl.when(has_to)(passed[p, k][0].wait_recv)

    def spread():
        for slot in range(4 * nf):
            source = slot // 2 if slot < 4 else 2 + slot % 2
            for i in range(4):
                if slot < 4:
                    row = w_tile[source, 4 * (slot % 2) + i : 4 * (slot % 2) + i + 1]
                else:
                    pair = (w_tile[source, i : i + 1], w_tile[source, 4 + i : 5 + i])
                    row = jnp.where((x == 0) == (slot < 6), pair[0], pair[1])
                wide = jnp.broadcast_to(row, (16, 128)).astype(BF16)
                w_buf[slot, i] = jnp.concatenate([wide] * (size // 128), axis=1)

    def mixture(p, columns, f):
        width = columns.stop - columns.start

        def term(i):
            block = green[p, i, :, columns].reshape(size // 16, 16, width)
            return w_buf[f, i, :, columns][None] * block

        return ((term(0) + term(1)) + (term(2) + term(3))).reshape(size, width)

    def left_side(p, columns, start, stop):
        def product(f, carry):
            left = jnp.dot(c_buf[f], mixture(p, columns, f), preferred_element_type=F32)
            left_buf[f, :, columns] = left.astype(BF16)
            return carry

        lax.fori_loop(start, stop, product, 0, unroll=min(UNROLL, stop - start))

    def right_side(columns, start, stop, rows=slice(None)):
        def beside(ref, rows):
            return jnp.concatenate([ref[f, rows, columns] for f in range(start, stop)], axis=1)

        return by_rows(beside(left_buf, rows), beside(c_buf, slice(None)))

    full = slice(0, size)
    halves = [pl.ds(h * half, half) for h in range(2)]
    for_edge = for_beside = for_sums
    to_across = [remote(edge_own.at[:, columns], edge_other.at[:, columns], across, for_edge) for columns in halves]
    to_beside = [remote(edge_own.at[:, columns], near_own.at[:, columns], opposite, for_beside) for columns in halves]
    for_over = for_under = group(edge_own)
    uneven = [pl.ds(0, size - size // 4), pl.ds(size - size // 4, size // 4)]
    over_across = [remote(near_own.at[rows, halves[1]], near_other.at[rows, halves[1]], across, for_over) for rows in uneven]
    over_beside = [remote(edge_other.at[rows, halves[0]], near_other.at[rows, halves[0]], opposite, for_under) for rows in uneven]
    for_comb = for_sums
    to_partner = [remote(comb.at[0, m, 0], comb.at[1, m, 0], partner, for_comb) for m in range(2)]
    late_to_partner = [remote(comb.at[0, 0, 1, rows], comb.at[1, 0, 1, rows], partner, for_comb) for rows in halves]
    last_to_partner = [remote(comb.at[0, 1, 1, rows], comb.at[1, 1, 1, rows], partner, for_comb) for rows in uneven]
    weight_outer, weight_edge = beside_weight[outer], beside_weight[edge]

    fill(0)
    came(w_in[1])
    go(w_on)
    pump(0)
    pass_on(0, 0)
    pump(1)
    came(w_in[0])
    came(w_on)
    spread()
    load_c.wait()
    load_own[0].wait()
    came(c_near)
    arrive(0, 0)
    left_side(0, parts[0], 0, 2)
    pump(2)
    left_side(0, parts[0], 2, 4)
    pump(3)
    acc[0] = right_side(parts[0], 0, 4)
    pump(4)
    pass_on(0, 1)
    pump(5)
    arrive(0, 1)
    left_side(0, parts[1], 0, 2)
    pump(6)
    left_side(0, parts[1], 2, 4)
    rest(0)
    acc[0] += right_side(parts[1], 0, 4)
    pass_on(1, 2)
    pl.when(has_from)(far[1, 2][0].wait_recv)
    go(near[2, 2])
    go(far[2, 2])
    for copy in c_far:
        came(copy)
    left_side(0, full, 4, 6)
    rest(1)
    rest(2)
    acc[0] += right_side(full, 4, 6)
    pass_on(1, 0)
    left_side(0, full, 6, 7)
    acc[0] += right_side(full, 6, 7)
    for copy in c_rest:
        came(copy)
    left_side(0, full, 7, 8)
    edge_own[...] = (acc[0] + right_side(full, 7, 8)).astype(BF16)
    go(to_across[0])
    go(to_beside[1])
    go(to_across[1])
    go(to_beside[0])

    fill(1)
    fill(2)
    for load in load_own[1:] + [load_r]:
        load.wait()
    rows = size // 4
    mine = pl.ds(pl.multiple_of(q * rows, rows), rows)
    here = y == 0
    for n, e in enumerate((core, 1 - core)):
        for m, s in enumerate((outer, edge)):
            real, imag = r_buf[e, s, 0, mine], r_buf[e, s, 1, mine]
            rows_of[n, m, 0] = jnp.concatenate([jnp.where(here, real, -imag), jnp.where(here, imag, real)], axis=0)
            rows_of[n, m, 1] = jnp.concatenate([jnp.where(here, -imag, real), jnp.where(here, real, imag)], axis=0)

    pass_on(2, 2)
    pl.when(has_to)(passed[1, 2][0].wait_recv)
    arrive(1, 0)
    left_side(1, parts[0], 0, 8)
    acc[1] = right_side(parts[0], 0, 8)
    pass_on(1, 1)
    arrive(1, 1)
    left_side(1, parts[1], 0, 8)
    total = acc[1] + right_side(parts[1], 0, 8)
    own = edge_own[...].astype(F32)
    comb[0, 0, 0] = (total + weight_outer * own).astype(BF16)
    go(to_partner[0])
    acc[1] = own + weight_edge * total
    came(to_beside[1])
    came(to_across[0])
    for r in range(2):
        go(over_across[r])
        go(over_beside[r])
    pass_on(2, 0)
    arrive(2, 2)
    arrive(2, 0)
    left_side(2, parts[0], 0, 8)
    acc[0] = right_side(parts[0], 0, 8)

    def project(n, m, c):
        return jnp.dot(rows_of[n, m, c], comb[n, m, c], preferred_element_type=F32)

    came(to_beside[0])
    comb[0, 1, 0] = (acc[1] + weight_edge * near_own[...].astype(F32)).astype(BF16)
    go(to_partner[1])
    pass_on(2, 1)
    for n in range(2):
        for m in range(2):
            if n == 1:
                came(to_partner[m])
            middle[n, m] = project(n, m, 0)
    came(to_across[1])
    arrive(2, 1)
    left_side(2, parts[1], 0, 8)
    for h, rows in enumerate(halves):
        acc[0, rows] += right_side(parts[1], 0, 8, rows)
        comb[0, 0, 1, rows] = (acc[0, rows] + weight_outer * edge_other[rows].astype(F32)).astype(BF16)
        go(late_to_partner[h])
    rows = size // 4

    def finish(*blocks):
        both = [(middle[n, m] + project(n, m, 1)).astype(BF16) for n, m in blocks]
        for (n, m), sums in zip(blocks, both):
            e, s = (core, 1 - core)[n], (outer, edge)[m]
            real, imag = sums[:rows], sums[rows:]
            sides = jnp.concatenate(
                [jnp.concatenate([real, imag], axis=1), jnp.concatenate([imag, -real], axis=1)], axis=0
            )
            updated = by_rows(sides, jnp.concatenate([r_buf[e, s, 0], r_buf[e, s, 1]], axis=1))
            out[e, s, 0] = updated[:rows]
            out[e, s, 1] = updated[rows:]

    def gather(r):
        came(over_across[r])
        came(over_beside[r])
        rows = uneven[r]
        around = acc[0, rows] + near_other[rows].astype(F32)
        comb[0, 1, 1, rows] = (edge_other[rows].astype(F32) + weight_edge * around).astype(BF16)
        go(last_to_partner[r])

    gather(0)
    finish((0, 0))
    gather(1)
    for copy in late_to_partner:
        came(copy)
    finish((0, 1), (1, 0))
    for copy in last_to_partner:
        came(copy)
    finish((1, 1))

    for n, (total, condition) in enumerate(groups):
        done = pltpu.make_async_remote_copy(
            src_ref=total, dst_ref=total, send_sem=send_sem.at[n], recv_sem=recv_sem.at[0],
            device_id=partner, device_id_type=MESH,
        )
        under(condition, done.wait_send)


def fast(lesser, retarded, coupling, occupations, offsets, intersection):
    nf, size, _ = coupling.shape
    rows = size // 4
    arrivals = 3 + 1 + 2 * len(RELAYS) + 2 + 5 + 6 * PIECES + 6 + 8 + 6
    anywhere = pl.BlockSpec(memory_space=pl.ANY)
    return pl.pallas_call(
        functools.partial(kernel, lax.axis_size("energy")),
        out_shape=pltpu.VMEM((2, 2, 2, rows, size), F32),
        in_specs=[anywhere] * 3 + [pl.BlockSpec(memory_space=pltpu.SMEM)] * 3,
        out_specs=pl.BlockSpec(memory_space=pltpu.VMEM),
        scratch_shapes=[
            pltpu.VMEM((PIECES, 4, size, size), BF16),
            pltpu.VMEM((4 * nf, size, size), BF16),
            pltpu.VMEM((4, 8, 128), F32),
            pltpu.VMEM((4 * nf, 4, 16, size), BF16),
            pltpu.VMEM((2, 2, 2, size, size), BF16),
            pltpu.VMEM((4 * nf, size, size), BF16),
            pltpu.VMEM((2, size, size), F32),
            pltpu.VMEM((size, size), BF16),
            pltpu.VMEM((size, size), BF16),
            pltpu.VMEM((size, size), BF16),
            pltpu.VMEM((size, size), BF16),
            pltpu.VMEM((2, 2, 2, size, size), BF16),
            pltpu.VMEM((2, 2, 2, 2 * rows, size), BF16),
            pltpu.VMEM((2, 2, 2 * rows, size), F32),
            pltpu.SemaphoreType.DMA((2 + PIECES,)),
            pltpu.SemaphoreType.DMA((GROUPS,)),
            pltpu.SemaphoreType.DMA((arrivals,)),
        ],
        compiler_params=pltpu.CompilerParams(
            collective_id=0, has_side_effects=True, vmem_limit_bytes=60 << 20
        ),
    )(lesser, retarded, coupling, occupations, offsets, intersection)


def solution(mesh):
    def shards(lesser, retarded, *rest):
        fits = (
            (mesh.shape["slab"], mesh.shape["freq"]) == (2, 4)
            and lesser.shape[:2] == (2, 2)
            and lesser.shape[-1] == 512
            and rest[0].shape[0] == 2
        )
        return (fast if fits else general)(lesser, retarded, *rest)

    return jax.shard_map(
        shards,
        mesh=mesh,
        in_specs=(
            P("energy", "slab", None, None, None),
            P("energy", "slab", None, None, None),
            P("freq", None, None),
            P("freq"),
            P("freq"),
            P("slab"),
        ),
        out_specs=P("energy", "slab", None, "freq", None),
        check_vma=False,
    )
```
